512 devices in a mesh: blk: 128 (over z, y, x_lo), rep: 4 (over x_hi, core).
Axes of the slice: x: 4 (x_hi: 2, x_lo: 2; x = x_hi * 2 + x_lo), y: 4, z: 16, core: 2. Of those that a mesh axis runs over, the one named last changes fastest.
Arguments:
- segment_ids: int32 [131072], P('rep'), parts along dimension 0, may hold values from 0 to 8191, as said below
- block_mask: int32 [512, 128], P('rep'), parts along dimension 0, may hold values from 0 to 1, as said below
- queries: bfloat16 [131072, 640], P(('rep', 'blk')), parts along dimension 0, may hold values from -256 to 256
- keys: bfloat16 [131072, 640], P(('rep', 'blk')), parts along dimension 0, may hold values from -8 to 8
- values: bfloat16 [131072, 640], P(('rep', 'blk')), parts along dimension 0, may hold values from -6 to 6
- tokens: bfloat16 [131072, 1280], P(('rep', 'blk')), parts along dimension 0, may hold values from -6 to 6
- out_weight: bfloat16 [640, 1280], replicated, may hold values from -6 to 6
- owners: int32 [32768], P(('rep', 'blk')), parts along dimension 0, may hold values from 0 to 127, as said below
- offsets: int32 [32768], P(('rep', 'blk')), parts along dimension 0, may hold values from 0 to 127, as said below
Outputs:
- received: bfloat16 [65536, 5120], P(('rep', 'blk')), parts along dimension 0
The draws below stay inside these ranges and needn't reach their ends.
There are 4 independent parts, one for each index of `rep`. The reference program is written for one: setup_inputs(seed, part) draws one part's arguments, and reference() takes and returns one part's arrays. A program takes and returns all parts, laid end to end along the dimension named above; an argument that names none is the same for every part. Nothing has to cross between parts.
Inputs may be any that keep to these rules, and one draw needn't show every extreme that they name: `segment_ids`: never falls; every segment has a multiple of 4 patches and at most 768. `block_mask`: 1 exactly where the two blocks share a segment id. `owners`: the merged rows of one block name one owner at most 2 times; each owner is named by at most 128 rows. Rows that name the same owner have distinct offsets.
All inputs are finite; a program needn't handle non-finite values.
Results may differ from the reference program's by a relative error of at most 0.0065.
Values may be sent and summed in bfloat16 or wider, within the bound.
A program may use at most 64 MiB of HBM per device.

```python
import jax
import jax.numpy as jnp
from jax import lax

D = 1280
HEADS = 8
HD = 80
TOK_DEV = 256
SPAN = 3
HF = 640
MERGED = 5120
NBLK = 128
TOKENS = 32768
SEGMAX = 768
MROWS = 64
CAP = 128
PAIR = 2


def segment_layout(key):
    quads = TOKENS // 4
    lengths = jax.random.randint(jax.random.fold_in(key, 11), (quads,), 1, SEGMAX // 4 + 1)
    lengths = lengths.at[0].set(1).at[1].set(SEGMAX // 4)
    bounds = jnp.cumsum(lengths)
    quad_seg = jnp.searchsorted(bounds, jnp.arange(quads), side='right').astype(jnp.int32)
    quad_seg = jnp.where(quad_seg == quad_seg[quads - 1], quads - 1, quad_seg).astype(jnp.int32)
    return jnp.repeat(quad_seg, 4)


def draw_segment_ids(key, part):
    return segment_layout(key)


def draw_block_mask(key, part):
    layout = segment_layout(key).reshape(NBLK, TOK_DEV)
    lowest = layout[:, 0]
    highest = layout[:, -1]
    joined = (lowest[:, None] <= highest[None, :]) & (lowest[None, :] <= highest[:, None])
    return joined.astype(jnp.int32)


def query_key_pair(key):
    query_draw = jax.random.truncated_normal(jax.random.fold_in(key, 21), -6.0, 6.0, (TOKENS, HEADS * HD), jnp.float32)
    key_draw = jax.random.truncated_normal(jax.random.fold_in(key, 22), -6.0, 6.0, (TOKENS, HEADS * HD), jnp.float32)
    return (query_draw, key_draw)


def draw_queries(key, part):
    return query_key_pair(key)[0].astype(jnp.bfloat16)


def draw_keys(key, part):
    return query_key_pair(key)[1].astype(jnp.bfloat16)


def owner_layout(key):
    total_rows = NBLK * MROWS
    entry = jnp.arange(total_rows)
    group = entry // (2 * CAP)
    within = entry % (2 * CAP)
    kind = (within >= CAP).astype(jnp.int32) + (within >= CAP + CAP // 2).astype(jnp.int32) + (within >= CAP + 3 * CAP // 4).astype(jnp.int32)
    starts = jnp.array([0, CAP, CAP + CAP // 2, CAP + 3 * CAP // 4], jnp.int32)
    slot = within - starts[kind]
    labels = jax.random.permutation(jax.random.fold_in(key, 31), NBLK).astype(jnp.int32)
    owner = labels[4 * group + kind]
    rotate = jax.random.randint(jax.random.fold_in(key, 32), (), 0, NBLK)
    unit = entry // PAIR
    sender = (unit + rotate) % NBLK
    local = unit // NBLK * PAIR + entry % PAIR
    orders = jax.vmap(lambda single: jax.random.permutation(single, MROWS))(jax.random.split(jax.random.fold_in(key, 33), NBLK))
    place = sender * MROWS + orders[sender, local]
    owners_out = jnp.zeros((total_rows,), jnp.int32).at[place].set(owner)
    offsets_out = jnp.zeros((total_rows,), jnp.int32).at[place].set(slot.astype(jnp.int32))
    return (owners_out, offsets_out)


def draw_owners(key, part):
    return owner_layout(key)[0]


def draw_offsets(key, part):
    return owner_layout(key)[1]


def levels(rng, extent, cuts, least, top_value):
    def one(axis_at, blocks):
        draws = jax.random.uniform(jax.random.fold_in(jax.random.fold_in(rng, 6), axis_at), (blocks,), jnp.float32, least / len(cuts), top_value / len(cuts))
        return jnp.repeat(jnp.exp(draws), extent[axis_at] // blocks).reshape((-1,) + (1,) * (len(extent) - axis_at - 1))

    gain = one(*cuts[0])
    for cut in cuts[1:]:
        gain = gain * one(*cut)
    return gain


def scatter_about(rng, shape, spread, reach, pieces=(), held_as=jnp.bfloat16):
    result = spread * jax.random.normal(rng, shape, jnp.float32)
    if pieces:
        result = result * levels(rng, shape, pieces, -0.22, 0.18)
    return jnp.clip(result, -reach, reach).astype(held_as)


def setup_inputs(seed: int = 0, part: int = 0) -> dict:
    key_of = jax.random.split(jax.random.key(seed), 10)
    own_keys = jax.random.split(jax.random.fold_in(key_of[9], part), 10)
    return {
        "segment_ids": draw_segment_ids(jax.random.fold_in(jax.random.fold_in(key_of[9], part), 71), part),
        "block_mask": draw_block_mask(jax.random.fold_in(jax.random.fold_in(key_of[9], part), 71), part),
        "queries": draw_queries(jax.random.fold_in(jax.random.fold_in(key_of[9], part), 71), part),
        "keys": draw_keys(jax.random.fold_in(jax.random.fold_in(key_of[9], part), 71), part),
        "values": scatter_about(own_keys[4], (TOKENS, HF), 1.0, 6.0, ((0, 128),)),
        "tokens": scatter_about(own_keys[5], (TOKENS, D), 0.5, 6.0, ((0, 128),)),
        "out_weight": scatter_about(key_of[6], (HF, D), 0.5, 6.0),
        "owners": draw_owners(jax.random.fold_in(jax.random.fold_in(key_of[9], part), 71), part),
        "offsets": draw_offsets(jax.random.fold_in(jax.random.fold_in(key_of[9], part), 71), part),
    }


NEG = -1e+30

def reference(segment_ids, block_mask, queries, keys, values, tokens, out_weight, owners, offsets):
    rows = TOK_DEV
    width = 2 * SPAN + 1
    hdim = queries.shape[1] // HEADS
    margin = SPAN * rows
    key_pad = jnp.pad(keys.astype(jnp.float32), ((margin, margin), (0, 0)))
    value_pad = jnp.pad(values.astype(jnp.float32), ((margin, margin), (0, 0)))
    seg_pad = jnp.pad(segment_ids, (margin, margin), constant_values=-1)
    mask_pad = jnp.pad(block_mask, ((0, 0), (SPAN, SPAN)))

    def one_block(index):
        start = index * rows
        query_block = lax.dynamic_slice_in_dim(queries, start, rows, 0).astype(jnp.float32).reshape(rows, HEADS, hdim)
        key_block = lax.dynamic_slice_in_dim(key_pad, start, width * rows, 0).reshape(width * rows, HEADS, hdim)
        value_block = lax.dynamic_slice_in_dim(value_pad, start, width * rows, 0).reshape(width * rows, HEADS, hdim)
        query_seg = lax.dynamic_slice_in_dim(segment_ids, start, rows, 0)
        key_seg = lax.dynamic_slice_in_dim(seg_pad, start, width * rows, 0)
        mask_row = lax.dynamic_index_in_dim(mask_pad, index, 0, keepdims=False)
        flags = jnp.repeat(lax.dynamic_slice_in_dim(mask_row, index, width, 0), rows)
        allowed = (query_seg[:, None] == key_seg[None, :]) & (flags[None, :] > 0)
        scores = jnp.einsum('rhd,khd->hrk', query_block, key_block) / jnp.sqrt(jnp.float32(hdim))
        scores = jnp.where(allowed[None], scores, NEG)
        peak = lax.optimization_barrier(jnp.max(scores, axis=2, keepdims=True))
        weights = jnp.where(allowed[None], jnp.exp(scores - peak), 0.0)
        total = lax.optimization_barrier(jnp.sum(weights, axis=2, keepdims=True))
        weights_low = lax.optimization_barrier(weights.astype(jnp.bfloat16)).astype(jnp.float32)
        mixed = jnp.einsum('hrk,khd->hrd', weights_low, value_block) / total
        return jnp.transpose(mixed, (1, 0, 2)).reshape(rows, HEADS * hdim).astype(jnp.bfloat16)
    attended = lax.map(one_block, jnp.arange(NBLK).astype(jnp.int32)).reshape(TOKENS, HEADS * hdim)
    hidden = (tokens.astype(jnp.float32) + jnp.dot(attended, out_weight, preferred_element_type=jnp.float32)).astype(jnp.bfloat16)
    merged = hidden.reshape(NBLK * MROWS, MERGED)
    target = (owners * CAP + offsets).astype(jnp.int32)
    return jnp.zeros((NBLK * CAP, MERGED), jnp.bfloat16).at[target].set(merged)
```

```python
import functools

import jax
import jax.numpy as jnp
from jax import lax
from jax.experimental import pallas as pl
from jax.experimental.pallas import tpu as pltpu
from jax.sharding import PartitionSpec as P

HEADS = 8
SPAN = 3
NEG = -1e30
LANES = 128


def halo_kernel(nblk, k_ref, v_ref, kh, vh, ksend, vsend, krecv, vrecv):
    me = lax.axis_index("blk")
    rungs = nblk // 2
    rung, side = lax.div(me, 2), lax.rem(me, 2)
    up = lax.rem(rung + 1, rungs) * 2 + side
    down = lax.rem(rung + rungs - 1, rungs) * 2 + side
    across = rung * 2 + 1 - side
    far = lax.rem(rung + 1 - 2 * side + rungs, rungs) * 2 + side

    barrier = pltpu.get_barrier_semaphore()
    for other in (up, down, across):
        pl.semaphore_signal(barrier, inc=1, device_id={"blk": other}, device_id_type=pl.DeviceIdType.MESH)
    pl.semaphore_wait(barrier, 3)

    def send(src, dst, sends, recvs, number, slot, target):
        copy = pltpu.make_async_remote_copy(
            src_ref=src,
            dst_ref=dst.at[slot],
            send_sem=sends.at[number],
            recv_sem=recvs.at[slot],
            device_id={"blk": target},
            device_id_type=pl.DeviceIdType.MESH,
        )
        copy.start()
        return copy

    def arrived(dst, recvs, slot):
        pltpu.make_async_copy(dst.at[slot], dst.at[slot], recvs.at[slot]).wait()

    started = []
    started.append(send(v_ref, vh, vsend, vrecv, 0, 2 + side, across))
    started.append(send(k_ref, kh, ksend, krecv, 1, 1, up))
    started.append(send(k_ref, kh, ksend, krecv, 2, 4, down))
    started.append(send(k_ref, kh, ksend, krecv, 0, 2 + side, across))
    started.append(send(v_ref, vh, vsend, vrecv, 1, 1, up))
    started.append(send(v_ref, vh, vsend, vrecv, 2, 4, down))
    arrived(vh, vrecv, 3 - side)
    started.append(send(vh.at[3 - side], vh, vsend, vrecv, 3, 2 - 2 * side, up))
    started.append(send(vh.at[3 - side], vh, vsend, vrecv, 4, 5 - 2 * side, down))
    arrived(kh, krecv, 1)
    started.append(send(kh.at[1], kh, ksend, krecv, 3, 2 * side, across))
    arrived(kh, krecv, 4)
    started.append(send(kh.at[4], kh, ksend, krecv, 4, 3 + 2 * side, across))
    arrived(kh, krecv, 2 - 2 * side)
    arrived(kh, krecv, 5 - 2 * side)
    started.append(send(kh.at[2 + side], kh, ksend, krecv, 5, 5 * side, far))
    arrived(vh, vrecv, 2 - 2 * side)
    arrived(vh, vrecv, 5 - 2 * side)
    started.append(send(vh.at[2 + side], vh, vsend, vrecv, 5, 5 * side, far))
    arrived(kh, krecv, 3 - side)
    arrived(vh, vrecv, 1)
    arrived(vh, vrecv, 4)
    arrived(kh, krecv, 5 * side)
    arrived(vh, vrecv, 5 * side)
    for copy in started:
        copy.wait_send()


def halo(keys, values, nblk):
    rows, features = keys.shape
    shape = jax.ShapeDtypeStruct((2 * SPAN, rows, features), keys.dtype)
    return pl.pallas_call(
        functools.partial(halo_kernel, nblk),
        out_shape=(shape, shape),
        in_specs=[pl.BlockSpec(memory_space=pl.ANY)] * 2,
        out_specs=(pl.BlockSpec(memory_space=pl.ANY),) * 2,
        scratch_shapes=[pltpu.SemaphoreType.DMA((6,))] * 4,
        compiler_params=pltpu.CompilerParams(collective_id=0, has_side_effects=True),
    )(keys, values)


def to_column(row):
    size = row.shape[1]
    diagonal = lax.broadcasted_iota(jnp.int32, (size, size), 0) == lax.broadcasted_iota(
        jnp.int32, (size, size), 1
    )
    return jnp.sum(jnp.where(diagonal, row, 0), axis=1, keepdims=True)


def attend_kernel(
    here, q_ref, k_ref, v_ref, kh, vh, seg_ref, mask_ref, tok_ref, w_ref, route_ref, out_ref, att
):
    rows, features = q_ref.shape
    nblk = seg_ref.shape[0]
    width = tok_ref.shape[1]
    hdim = features // HEADS
    block = here[0]
    scale = 1.0 / jnp.sqrt(jnp.float32(hdim))
    query_seg = to_column(seg_ref[pl.ds(block, 1), :])
    mask_row = mask_ref[pl.ds(block, 1), :]
    columns = lax.broadcasted_iota(jnp.int32, mask_row.shape, 1)
    key_segs, sources = [], []
    for dist in range(-SPAN, SPAN + 1):
        column = block + dist
        flag = jnp.sum(jnp.where(columns == column, mask_row, 0), axis=1, keepdims=True)
        ids = seg_ref[pl.ds(jnp.clip(column, 0, nblk - 1), 1), :]
        key_segs.append(jnp.where(flag > 0, ids, -1))
        if dist == 0:
            sources.append((k_ref, v_ref))
        else:
            slot = dist + SPAN - (1 if dist > 0 else 0)
            sources.append((kh.at[slot], vh.at[slot]))
    for head in range(HEADS):
        first, last = head * hdim, (head + 1) * hdim
        low = first // LANES * LANES
        high = -(-last // LANES) * LANES
        lane = lax.broadcasted_iota(jnp.int32, (rows, high - low), 1) + low
        mine = (lane >= first) & (lane < last)
        query = jnp.where(mine, q_ref[:, low:high], jnp.bfloat16(0))
        scores = []
        for (key, _), key_seg in zip(sources, key_segs):
            part = lax.dot_general(
                query, key[:, low:high], (((1,), (1,)), ((), ())), preferred_element_type=jnp.float32
            )
            scores.append(jnp.where(query_seg == key_seg, part, NEG))
        peak = functools.reduce(jnp.maximum, scores)
        peak = jnp.max(peak, axis=1, keepdims=True)
        total = jnp.zeros((rows, 1), jnp.float32)
        mixed = jnp.zeros((rows, high - low), jnp.float32)
        for (_, value), part in zip(sources, scores):
            weights = jnp.exp((part - peak) * scale)
            total = total + jnp.sum(weights, axis=1, keepdims=True)
            mixed = mixed + jnp.dot(
                weights.astype(jnp.bfloat16), value[:, low:high], preferred_element_type=jnp.float32
            )
        att[:, low:high] = jnp.where(mine, mixed / total, att[:, low:high])
    hidden = (
        tok_ref[...].astype(jnp.float32)
        + jnp.dot(att[...].astype(jnp.bfloat16), w_ref[...], preferred_element_type=jnp.float32)
    ).astype(jnp.bfloat16)
    owner_row = route_ref[0:1, :]
    owner_col = to_column(owner_row)
    down = lax.broadcasted_iota(jnp.int32, (rows, rows), 0)
    right = lax.broadcasted_iota(jnp.int32, (rows, rows), 1)
    earlier = (owner_col == owner_row) & (down < right // 4 * 4) & (down % 4 == 0)
    rank = jnp.sum(earlier.astype(jnp.int32), axis=0, keepdims=True)
    slot = 2 * owner_row + rank
    hit = down == slot
    for quarter in range(4):
        pick = (hit & (right % 4 == quarter)).astype(jnp.float32)
        if quarter == 0:
            offset = jnp.sum(pick * route_ref[1:2, :].astype(jnp.float32), axis=1, keepdims=True)
            used = jnp.sum(pick, axis=1, keepdims=True)
            offset = jnp.where(used > 0, offset, 2.0 * nblk)
            out_ref[:, 4 * width :] = jnp.broadcast_to(offset, (rows, LANES)).astype(jnp.bfloat16)
        out_ref[:, quarter * width : (quarter + 1) * width] = jnp.dot(
            pick.astype(jnp.bfloat16), hidden, preferred_element_type=jnp.float32
        ).astype(jnp.bfloat16)


def place_kernel(in_ref, out_ref):
    slots = in_ref.shape[0]
    rows, width = out_ref.shape
    tag = in_ref[:, width:].astype(jnp.float32)[:, 0:1]
    down = lax.broadcasted_iota(jnp.int32, (slots, slots), 0)
    right = lax.broadcasted_iota(jnp.int32, (slots, slots), 1)
    tag = jnp.sum(jnp.where(down == right, tag, 0.0), axis=0, keepdims=True)
    spot = lax.broadcasted_iota(jnp.int32, (rows, slots), 0).astype(jnp.float32)
    pick = jnp.where(spot == tag, 1.0, 0.0).astype(jnp.bfloat16)
    step = width // 4
    for start in range(0, width, step):
        out_ref[:, start : start + step] = jnp.dot(
            pick, in_ref[:, start : start + step], preferred_element_type=jnp.float32
        ).astype(jnp.bfloat16)


def per_device(segment_ids, block_mask, queries, keys, values, tokens, out_weight, owners, offsets):
    rows = queries.shape[0]
    width = tokens.shape[1]
    nblk = lax.axis_size("blk")
    mrows = rows // 4
    capacity = 2 * mrows
    wide = 4 * width + LANES
    key_halo, value_halo = halo(keys, values, nblk)
    here = lax.axis_index("blk").reshape(1)
    route = jnp.broadcast_to(jnp.stack([owners, offsets])[:, :, None], (2, mrows, 4)).reshape(2, rows)
    vmem = pl.BlockSpec(memory_space=pltpu.VMEM)
    outgoing = pl.pallas_call(
        attend_kernel,
        out_shape=jax.ShapeDtypeStruct((2 * nblk, wide), jnp.bfloat16),
        in_specs=[pl.BlockSpec(memory_space=pltpu.SMEM)] + [vmem] * 10,
        out_specs=vmem,
        scratch_shapes=[pltpu.VMEM(queries.shape, jnp.float32)],
        compiler_params=pltpu.CompilerParams(vmem_limit_bytes=48 * 2**20),
    )(
        here,
        queries,
        keys,
        values,
        key_halo,
        value_halo,
        segment_ids.reshape(nblk, rows),
        block_mask,
        tokens,
        out_weight,
        route,
    )
    arrived = lax.all_to_all(
        outgoing.reshape(nblk, 2, wide), "blk", split_axis=0, concat_axis=0, tiled=True
    )
    return pl.pallas_call(
        place_kernel,
        out_shape=jax.ShapeDtypeStruct((capacity, 4 * width), jnp.bfloat16),
        in_specs=[vmem],
        out_specs=vmem,
    )(arrived.reshape(2 * nblk, wide))


def solution(mesh):
    placed = (
        P("rep"),
        P("rep", None),
        P(("rep", "blk"), None),
        P(("rep", "blk"), None),
        P(("rep", "blk"), None),
        P(("rep", "blk"), None),
        P(),
        P(("rep", "blk")),
        P(("rep", "blk")),
    )
    return jax.shard_map(
        per_device, mesh=mesh, in_specs=placed, out_specs=P(("rep", "blk"), None), check_vma=False
    )
```

```python
import functools

import jax
import jax.numpy as jnp
from jax import lax
from jax.experimental import pallas as pl
from jax.experimental.pallas import tpu as pltpu
from jax.sharding import PartitionSpec as P

HEADS = 8
SPAN = 3
NEG = -1e30
LANES = 128
PLANE = 8
REACH = 4
CHUNKS = 4


def halo_kernel(nblk, k_ref, v_ref, kh, vh, ksend, vsend, krecv, vrecv):
    me = lax.axis_index("blk")
    rungs = nblk // 2
    rung, side = lax.div(me, 2), lax.rem(me, 2)
    up = lax.rem(rung + 1, rungs) * 2 + side
    down = lax.rem(rung + rungs - 1, rungs) * 2 + side
    across = rung * 2 + 1 - side
    far = lax.rem(rung + 1 - 2 * side + rungs, rungs) * 2 + side

    barrier = pltpu.get_barrier_semaphore()
    for other in (up, down, across):
        pl.semaphore_signal(barrier, inc=1, device_id={"blk": other}, device_id_type=pl.DeviceIdType.MESH)
    pl.semaphore_wait(barrier, 3)

    def send(src, dst, sends, recvs, number, slot, target):
        copy = pltpu.make_async_remote_copy(
            src_ref=src,
            dst_ref=dst.at[slot],
            send_sem=sends.at[number],
            recv_sem=recvs.at[slot],
            device_id={"blk": target},
            device_id_type=pl.DeviceIdType.MESH,
        )
        copy.start()
        return copy

    def arrived(dst, recvs, slot):
        pltpu.make_async_copy(dst.at[slot], dst.at[slot], recvs.at[slot]).wait()

    started = []
    started.append(send(v_ref, vh, vsend, vrecv, 0, 2 + side, across))
    started.append(send(k_ref, kh, ksend, krecv, 1, 1, up))
    started.append(send(k_ref, kh, ksend, krecv, 2, 4, down))
    started.append(send(k_ref, kh, ksend, krecv, 0, 2 + side, across))
    started.append(send(v_ref, vh, vsend, vrecv, 1, 1, up))
    started.append(send(v_ref, vh, vsend, vrecv, 2, 4, down))
    arrived(vh, vrecv, 3 - side)
    started.append(send(vh.at[3 - side], vh, vsend, vrecv, 3, 2 - 2 * side, up))
    started.append(send(vh.at[3 - side], vh, vsend, vrecv, 4, 5 - 2 * side, down))
    arrived(kh, krecv, 1)
    started.append(send(kh.at[1], kh, ksend, krecv, 3, 2 * side, across))
    arrived(kh, krecv, 4)
    started.append(send(kh.at[4], kh, ksend, krecv, 4, 3 + 2 * side, across))
    arrived(kh, krecv, 2 - 2 * side)
    arrived(kh, krecv, 5 - 2 * side)
    started.append(send(kh.at[2 + side], kh, ksend, krecv, 5, 5 * side, far))
    arrived(vh, vrecv, 2 - 2 * side)
    arrived(vh, vrecv, 5 - 2 * side)
    started.append(send(vh.at[2 + side], vh, vsend, vrecv, 5, 5 * side, far))
    arrived(kh, krecv, 3 - side)
    arrived(vh, vrecv, 1)
    arrived(vh, vrecv, 4)
    arrived(kh, krecv, 5 * side)
    arrived(vh, vrecv, 5 * side)
    for copy in started:
        copy.wait_send()


def halo(keys, values, nblk):
    rows, features = keys.shape
    shape = jax.ShapeDtypeStruct((2 * SPAN, rows, features), keys.dtype)
    return pl.pallas_call(
        functools.partial(halo_kernel, nblk),
        out_shape=(shape, shape),
        in_specs=[pl.BlockSpec(memory_space=pl.ANY)] * 2,
        out_specs=(pl.BlockSpec(memory_space=pl.ANY),) * 2,
        scratch_shapes=[pltpu.SemaphoreType.DMA((6,))] * 4,
        compiler_params=pltpu.CompilerParams(collective_id=0, has_side_effects=True),
    )(keys, values)


def to_column(row):
    size = row.shape[1]
    diagonal = lax.broadcasted_iota(jnp.int32, (size, size), 0) == lax.broadcasted_iota(
        jnp.int32, (size, size), 1
    )
    return jnp.sum(jnp.where(diagonal, row, 0), axis=1, keepdims=True)


def attend_kernel(
    here, q_ref, k_ref, v_ref, kh, vh, seg_ref, mask_ref, tok_ref, w_ref, route_ref, out_ref, att
):
    rows, features = q_ref.shape
    nblk = seg_ref.shape[0]
    width = tok_ref.shape[1]
    hdim = features // HEADS
    block = here[0]
    scale = 1.0 / jnp.sqrt(jnp.float32(hdim))
    query_seg = to_column(seg_ref[pl.ds(block, 1), :])
    mask_row = mask_ref[pl.ds(block, 1), :]
    columns = lax.broadcasted_iota(jnp.int32, mask_row.shape, 1)
    key_segs, sources = [], []
    for dist in range(-SPAN, SPAN + 1):
        column = block + dist
        flag = jnp.sum(jnp.where(columns == column, mask_row, 0), axis=1, keepdims=True)
        ids = seg_ref[pl.ds(jnp.clip(column, 0, nblk - 1), 1), :]
        key_segs.append(jnp.where(flag > 0, ids, -1))
        if dist == 0:
            sources.append((k_ref, v_ref))
        else:
            slot = dist + SPAN - (1 if dist > 0 else 0)
            sources.append((kh.at[slot], vh.at[slot]))
    for head in range(HEADS):
        first, last = head * hdim, (head + 1) * hdim
        low = first // LANES * LANES
        high = -(-last // LANES) * LANES
        lane = lax.broadcasted_iota(jnp.int32, (rows, high - low), 1) + low
        mine = (lane >= first) & (lane < last)
        query = jnp.where(mine, q_ref[:, low:high], jnp.bfloat16(0))
        scores = []
        for (key, _), key_seg in zip(sources, key_segs):
            part = lax.dot_general(
                query, key[:, low:high], (((1,), (1,)), ((), ())), preferred_element_type=jnp.float32
            )
            scores.append(jnp.where(query_seg == key_seg, part, NEG))
        peak = functools.reduce(jnp.maximum, scores)
        peak = jnp.max(peak, axis=1, keepdims=True)
        total = jnp.zeros((rows, 1), jnp.float32)
        mixed = jnp.zeros((rows, high - low), jnp.float32)
        for (_, value), part in zip(sources, scores):
            weights = jnp.exp((part - peak) * scale)
            total = total + jnp.sum(weights, axis=1, keepdims=True)
            mixed = mixed + jnp.dot(
                weights.astype(jnp.bfloat16), value[:, low:high], preferred_element_type=jnp.float32
            )
        att[:, low:high] = jnp.where(mine, mixed / total, att[:, low:high])
    hidden = (
        tok_ref[...].astype(jnp.float32)
        + jnp.dot(att[...].astype(jnp.bfloat16), w_ref[...], preferred_element_type=jnp.float32)
    ).astype(jnp.bfloat16)
    owner_row = route_ref[0:1, :]
    owner_col = to_column(owner_row)
    down = lax.broadcasted_iota(jnp.int32, (rows, rows), 0)
    right = lax.broadcasted_iota(jnp.int32, (rows, rows), 1)
    earlier = (owner_col == owner_row) & (down < right // 4 * 4) & (down % 4 == 0)
    rank = jnp.sum(earlier.astype(jnp.int32), axis=0, keepdims=True)
    slot = 2 * owner_row + rank
    mrows = rows // 4
    merged = lax.broadcasted_iota(jnp.int32, (mrows, rows), 0)
    source = lax.broadcasted_iota(jnp.int32, (mrows, rows), 1)
    lane = lax.broadcasted_iota(jnp.int32, (mrows, LANES), 1)
    for quarter in range(4):
        pick = source == 4 * merged + quarter
        if quarter == 0:
            offset = jnp.sum(jnp.where(pick, route_ref[1:2, :], 0), axis=1, keepdims=True)
            code = jnp.sum(jnp.where(pick, slot, 0), axis=1, keepdims=True)
            tags = jnp.where(lane < LANES // 2, offset + 1, code + 1)
            out_ref[:, :LANES] = tags.astype(jnp.float32).astype(jnp.bfloat16)
        start = LANES + quarter * width
        out_ref[:, start : start + width] = jnp.dot(
            pick.astype(jnp.float32).astype(jnp.bfloat16), hidden, preferred_element_type=jnp.float32
        ).astype(jnp.bfloat16)


def to_row(column):
    size = column.shape[0]
    diagonal = lax.broadcasted_iota(jnp.int32, (size, size), 0) == lax.broadcasted_iota(
        jnp.int32, (size, size), 1
    )
    return jnp.sum(jnp.where(diagonal, column, 0.0), axis=0, keepdims=True)


def codes_of(tags):
    return to_row(tags.astype(jnp.float32)[:, LANES // 2 : LANES // 2 + 1])


def as_onehot(hit):
    return jnp.where(hit, 1.0, 0.0).astype(jnp.bfloat16)


def pick_rows(onehot, rows):
    return jnp.dot(onehot, rows, preferred_element_type=jnp.float32)


def route_kernel(
    nblk, r_ref, out_ref, near, comp, far, ordered, landed, nsend, nrecv, fsend, frecv, psend, precv
):
    me = lax.axis_index("blk")
    planes = nblk // PLANE
    plane, spot = lax.div(me, PLANE), lax.rem(me, PLANE)
    mrows, wide = r_ref.shape
    per = 2 * PLANE
    step = (wide - LANES) // CHUNKS
    chunks = [(0, LANES + step)] + [(LANES + c * step, step) for c in range(1, CHUNKS)]

    def along(distance):
        return lax.rem(plane + distance + planes, planes) * PLANE + spot

    def within(distance):
        return plane * PLANE + lax.rem(spot + distance, PLANE)

    barrier = pltpu.get_barrier_semaphore()
    peers = [along(d) for k in range(1, REACH + 1) for d in (k, -k)]
    peers += [within(d) for d in range(1, PLANE)]
    for other in peers:
        pl.semaphore_signal(barrier, inc=1, device_id={"blk": other}, device_id_type=pl.DeviceIdType.MESH)
    pl.semaphore_wait(barrier, len(peers))

    started = []

    def send(src, dst, sends, recvs, number, target):
        copy = pltpu.make_async_remote_copy(
            src_ref=src,
            dst_ref=dst,
            send_sem=sends.at[number],
            recv_sem=recvs.at[number],
            device_id={"blk": target},
            device_id_type=pl.DeviceIdType.MESH,
        )
        copy.start()
        started.append(copy)
        return copy

    def near_at(way, hop):
        return (way * REACH + hop - 1) * mrows

    def forward(way, hop, chunk):
        begin, size = chunks[chunk]
        cols = pl.ds(begin, size)
        src = r_ref.at[:, cols] if hop == 1 else near.at[pl.ds(near_at(way, hop - 1), mrows), cols]
        return send(
            src,
            near.at[pl.ds(near_at(way, hop), mrows), cols],
            nsend,
            nrecv,
            (way * REACH + hop - 1) * CHUNKS + chunk,
            along(1 - 2 * way),
        )

    hops = {}
    for chunk in range(CHUNKS):
        for way in range(2):
            hops[way, 1, chunk] = forward(way, 1, chunk)
    for hop in range(1, REACH):
        for chunk in range(CHUNKS):
            for way in range(2):
                hops[way, hop, chunk].wait_recv()
                hops[way, hop + 1, chunk] = forward(way, hop + 1, chunk)

    def far_at(way, ahead):
        return (way * (REACH - 1) + ahead - 1) * per if ahead < REACH else 2 * (REACH - 1) * per

    relays, onehots = {}, {}
    for chunk, (begin, size) in enumerate(chunks):
        for way in range(2):
            hops[way, REACH, chunk].wait_recv()
            held = near_at(way, REACH)
            if chunk == 0:
                code = codes_of(near[held : held + mrows, :LANES])
                index = lax.broadcasted_iota(jnp.int32, (REACH * per, mrows), 0)
                ahead = index // per + 1
                goal = plane + (ahead if way == 0 else planes - ahead)
                goal = jnp.where(goal >= planes, goal - planes, goal)
                want = goal * per + index % per + 1
                onehots[way] = as_onehot(code == want.astype(jnp.float32))
            comp[way * REACH * per : (way + 1) * REACH * per, begin : begin + size] = pick_rows(
                onehots[way], near[held : held + mrows, begin : begin + size]
            ).astype(jnp.bfloat16)
            for ahead in range(REACH, 0, -1):
                if ahead == REACH and chunk * 2 // CHUNKS != way:
                    continue
                relays[way, ahead, chunk] = send(
                    comp.at[pl.ds((way * REACH + ahead - 1) * per, per), pl.ds(begin, size)],
                    far.at[pl.ds(far_at(way, ahead), per), pl.ds(begin, size)],
                    fsend,
                    frecv,
                    (way * REACH + ahead - 1) * CHUNKS + chunk,
                    along(ahead - 2 * way * ahead),
                )

    slots = per * planes
    each = slots // PLANE

    def wanted(columns):
        index = lax.broadcasted_iota(jnp.int32, (slots, columns), 0)
        column = lax.broadcasted_iota(jnp.int32, (slots, columns), 1)
        return index % each // 2, index // each * 2 + index % 2, column

    base = plane * per + 1
    group, local, column = wanted(mrows)
    code = codes_of(r_ref[:, :LANES])
    own_hot = as_onehot((group == 0) & (code == (local + base).astype(jnp.float32)))
    group, local, column = wanted(2 * REACH * mrows)
    code = codes_of(near[:, :LANES])
    near_hot = as_onehot(
        (group == 1 + column // mrows) & (code == (local + base).astype(jnp.float32))
    )
    group, local, column = wanted(far.shape[0])
    far_hot = as_onehot((group == 1 + 2 * REACH + column // per) & (local == column % per))

    spread = {}
    mine = pl.ds(pl.multiple_of(spot * each, each), each)
    for chunk, (begin, size) in enumerate(chunks):
        cols = slice(begin, begin + size)
        found = pick_rows(own_hot, r_ref[:, cols]) + pick_rows(near_hot, near[:, cols])
        for way in range(2):
            for ahead in range(1, REACH + 1):
                if (way, ahead, chunk) in relays:
                    relays[way, ahead, chunk].wait_recv()
        ordered[:, cols] = (found + pick_rows(far_hot, far[:, cols])).astype(jnp.bfloat16)
        for distance in range(1, PLANE):
            theirs = pl.ds(pl.multiple_of(lax.rem(spot + distance, PLANE) * each, each), each)
            spread[distance, chunk] = send(
                ordered.at[theirs, pl.ds(begin, size)],
                landed.at[mine, pl.ds(begin, size)],
                psend,
                precv,
                (distance - 1) * CHUNKS + chunk,
                within(distance),
            )
        landed[mine, cols] = ordered[mine, cols]

    for chunk, (begin, size) in enumerate(chunks):
        for distance in range(1, PLANE):
            spread[distance, chunk].wait_recv()
        if chunk == 0:
            tag = to_row(landed[:, :LANES].astype(jnp.float32)[:, 0:1])
            index = lax.broadcasted_iota(jnp.int32, (out_ref.shape[0], slots), 0) + 1
            place = as_onehot(index.astype(jnp.float32) == tag)
            begin, size = begin + LANES, size - LANES
        out_ref[:, begin - LANES : begin - LANES + size] = pick_rows(
            place, landed[:, begin : begin + size]
        ).astype(jnp.bfloat16)
    for copy in started:
        copy.wait_send()


def route_rows(rows, nblk, capacity):
    mrows, wide = rows.shape
    per = 2 * PLANE
    vmem = pl.BlockSpec(memory_space=pltpu.VMEM)
    dma = pltpu.SemaphoreType.DMA
    return pl.pallas_call(
        functools.partial(route_kernel, nblk),
        out_shape=jax.ShapeDtypeStruct((capacity, wide - LANES), rows.dtype),
        in_specs=[vmem],
        out_specs=vmem,
        scratch_shapes=[
            pltpu.VMEM((2 * REACH * mrows, wide), rows.dtype),
            pltpu.VMEM((2 * REACH * per, wide), rows.dtype),
            pltpu.VMEM(((2 * REACH - 1) * per, wide), rows.dtype),
            pltpu.VMEM((2 * nblk, wide), rows.dtype),
            pltpu.VMEM((2 * nblk, wide), rows.dtype),
        ]
        + [dma((2 * REACH * CHUNKS,))] * 4
        + [dma(((PLANE - 1) * CHUNKS,))] * 2,
        compiler_params=pltpu.CompilerParams(
            collective_id=1, has_side_effects=True, vmem_limit_bytes=48 * 2**20
        ),
    )(rows)


def per_device(segment_ids, block_mask, queries, keys, values, tokens, out_weight, owners, offsets):
    rows = queries.shape[0]
    width = tokens.shape[1]
    nblk = lax.axis_size("blk")
    mrows = rows // 4
    capacity = 2 * mrows
    wide = 4 * width + LANES
    key_halo, value_halo = halo(keys, values, nblk)
    here = lax.axis_index("blk").reshape(1)
    route = jnp.broadcast_to(jnp.stack([owners, offsets])[:, :, None], (2, mrows, 4)).reshape(2, rows)
    vmem = pl.BlockSpec(memory_space=pltpu.VMEM)
    outgoing = pl.pallas_call(
        attend_kernel,
        out_shape=jax.ShapeDtypeStruct((mrows, wide), jnp.bfloat16),
        in_specs=[pl.BlockSpec(memory_space=pltpu.SMEM)] + [vmem] * 10,
        out_specs=vmem,
        scratch_shapes=[pltpu.VMEM(queries.shape, jnp.float32)],
        compiler_params=pltpu.CompilerParams(vmem_limit_bytes=48 * 2**20),
    )(
        here,
        queries,
        keys,
        values,
        key_halo,
        value_halo,
        segment_ids.reshape(nblk, rows),
        block_mask,
        tokens,
        out_weight,
        route,
    )
    return route_rows(outgoing, nblk, capacity)


def solution(mesh):
    placed = (
        P("rep"),
        P("rep", None),
        P(("rep", "blk"), None),
        P(("rep", "blk"), None),
        P(("rep", "blk"), None),
        P(("rep", "blk"), None),
        P(),
        P(("rep", "blk")),
        P(("rep", "blk")),
    )
    return jax.shard_map(
        per_device, mesh=mesh, in_specs=placed, out_specs=P(("rep", "blk"), None), check_vma=False
    )
```

```python
import functools

import jax
import jax.numpy as jnp
from jax import lax
from jax.experimental import pallas as pl
from jax.experimental.pallas import tpu as pltpu
from jax.sharding import PartitionSpec as P

HEADS = 8
SPAN = 3
NEG = -1e30
LANES = 128
PLANE = 8
REACH = 4
CHUNKS = 4
PARTS = 2


def to_column(row):
    size = row.shape[1]
    diagonal = lax.broadcasted_iota(jnp.int32, (size, size), 0) == lax.broadcasted_iota(
        jnp.int32, (size, size), 1
    )
    return jnp.sum(jnp.where(diagonal, row, 0), axis=1, keepdims=True)


def attend_kernel(
    q_hbm, k_hbm, v_hbm, seg_hbm, mask_hbm, tok_hbm, w_hbm, route_hbm, out_ref,
    q_ref, k_ref, v_ref, seg_ref, mask_ref, tok_ref, w_ref, route_ref,
    kh, vh, peaks, totals, mixed, loads, ksend, vsend, krecv, vrecv,
):
    rows, features = q_ref.shape
    nblk = seg_ref.shape[0]
    width = tok_ref.shape[1]
    hdim = features // HEADS
    block = lax.axis_index("blk")
    scale = 1.0 / jnp.sqrt(jnp.float32(hdim))

    pairs = [
        (q_hbm, q_ref),
        (k_hbm, k_ref),
        (v_hbm, v_ref),
        (seg_hbm, seg_ref),
        (mask_hbm, mask_ref),
        (route_hbm, route_ref),
        (tok_hbm, tok_ref),
        (w_hbm, w_ref),
    ]
    local = [pltpu.make_async_copy(src, dst, loads.at[n]) for n, (src, dst) in enumerate(pairs)]
    for copy in local:
        copy.start()

    rungs = nblk // 2
    rung, side = lax.div(block, 2), lax.rem(block, 2)
    up = lax.rem(rung + 1, rungs) * 2 + side
    down = lax.rem(rung + rungs - 1, rungs) * 2 + side
    across = rung * 2 + 1 - side
    far = lax.rem(rung + 1 - 2 * side + rungs, rungs) * 2 + side
    back = lax.rem(rung - 1 + 2 * side + rungs, rungs) * 2 + side

    barrier = pltpu.get_barrier_semaphore()
    for other in (up, down, across):
        pl.semaphore_signal(barrier, inc=1, device_id={"blk": other}, device_id_type=pl.DeviceIdType.MESH)
    pl.semaphore_wait(barrier, 3)

    half = rows // PARTS
    started = []

    def send(src, dst, sends, recvs, number, slot, part, target):
        span = pl.ds(part * half, half)
        copy = pltpu.make_async_remote_copy(
            src_ref=src.at[span],
            dst_ref=dst.at[slot, span],
            send_sem=sends.at[number * PARTS + part],
            recv_sem=recvs.at[slot * PARTS + part],
            device_id={"blk": target},
            device_id_type=pl.DeviceIdType.MESH,
        )
        copy.start()
        started.append(copy)

    def arrived(dst, recvs, slot, part):
        span = pl.ds(part * half, half)
        pltpu.make_async_copy(
            dst.at[slot, span], dst.at[slot, span], recvs.at[slot * PARTS + part]
        ).wait()

    for part in range(PARTS):
        send(v_hbm, vh, vsend, vrecv, 0, 2 + side, part, across)
        send(k_hbm, kh, ksend, krecv, 1, 4 - 3 * side, part, back)
        send(k_hbm, kh, ksend, krecv, 2, 1 + 3 * side, part, far)
    for part in range(PARTS):
        send(k_hbm, kh, ksend, krecv, 0, 2 + side, part, across)
        send(v_hbm, vh, vsend, vrecv, 2, 1 + 3 * side, part, far)
        send(v_hbm, vh, vsend, vrecv, 1, 4 - 3 * side, part, back)
    for part in range(PARTS):
        arrived(vh, vrecv, 3 - side, part)
        send(vh.at[3 - side], vh, vsend, vrecv, 3, 2 + side, part, far)
        send(vh.at[3 - side], vh, vsend, vrecv, 4, 5 - 5 * side, part, back)
    for part in range(PARTS):
        arrived(kh, krecv, 4 - 3 * side, part)
        send(kh.at[4 - 3 * side], kh, ksend, krecv, 3, 3 - side, part, across)
    for part in range(PARTS):
        arrived(kh, krecv, 1 + 3 * side, part)
        send(kh.at[1 + 3 * side], kh, ksend, krecv, 4, 5 * side, part, across)

    for copy in local:
        copy.wait()
    query_seg = to_column(seg_ref[pl.ds(block, 1), :])
    mask_row = mask_ref[pl.ds(block, 1), :]
    columns = lax.broadcasted_iota(jnp.int32, mask_row.shape, 1)

    def segments(dist):
        column = block + dist
        flag = jnp.sum(jnp.where(columns == column, mask_row, 0), axis=1, keepdims=True)
        ids = seg_ref[pl.ds(lax.rem(column + nblk, nblk), 1), :]
        return jnp.where(flag > 0, ids, -1)

    def window(head):
        first, last = head * hdim, (head + 1) * hdim
        low, high = first // LANES * LANES, -(-last // LANES) * LANES
        lane = lax.broadcasted_iota(jnp.int32, (rows, high - low), 1) + low
        return low, high, (lane >= first) & (lane < last)

    def attend(blocks, fresh):
        for head in range(HEADS):
            low, high, mine = window(head)
            query = jnp.where(mine, q_ref[:, low:high], jnp.bfloat16(0))
            scores = []
            for key, _, key_seg in blocks:
                part = lax.dot_general(
                    query,
                    key[:, low:high],
                    (((1,), (1,)), ((), ())),
                    preferred_element_type=jnp.float32,
                )
                scores.append(jnp.where(query_seg == key_seg, part, NEG))
            peak = jnp.max(functools.reduce(jnp.maximum, scores), axis=1, keepdims=True)
            if fresh:
                total = jnp.zeros((rows, 1), jnp.float32)
                result = jnp.zeros((rows, high - low), jnp.float32)
            else:
                before = peaks[head]
                peak = jnp.maximum(peak, before)
                factor = jnp.exp((before - peak) * scale)
                total = totals[head] * factor
                result = mixed[head, :, : high - low] * factor
            for (_, value, _), part in zip(blocks, scores):
                weights = jnp.exp((part - peak) * scale)
                total = total + jnp.sum(weights, axis=1, keepdims=True)
                result = result + jnp.dot(
                    weights.astype(jnp.bfloat16), value[:, low:high], preferred_element_type=jnp.float32
                )
            peaks[head] = peak
            totals[head] = total
            mixed[head, :, : high - low] = result

    def held(slot, dist):
        return kh.at[slot], vh.at[slot], segments(dist)

    for part in range(PARTS):
        arrived(kh, krecv, 3 - side, part)
        arrived(vh, vrecv, 1, part)
        arrived(vh, vrecv, 4, part)
    attend(
        [(k_ref, v_ref, segments(0)), held(3 - side, 1 - 2 * side), held(1, -2), held(4, 2)], True
    )
    for part in range(PARTS):
        arrived(vh, vrecv, 2 + side, part)
        send(vh.at[2 + side], vh, vsend, vrecv, 5, 5 * side, part, far)
    for part in range(PARTS):
        arrived(kh, krecv, 2 + side, part)
        send(kh.at[2 + side], kh, ksend, krecv, 5, 5 * side, part, far)
    for part in range(PARTS):
        arrived(vh, vrecv, 5 - 5 * side, part)
        arrived(kh, krecv, 5 - 5 * side, part)
    attend([held(2 + side, 2 * side - 1), held(5 - 5 * side, 3 - 6 * side)], False)
    for part in range(PARTS):
        arrived(vh, vrecv, 5 * side, part)
        arrived(kh, krecv, 5 * side, part)
    attend([held(5 * side, 6 * side - 3)], False)

    pieces = []
    for group in range(features // LANES):
        piece = jnp.zeros((rows, LANES), jnp.float32)
        for head in range(HEADS):
            low, high, mine = window(head)
            start = group * LANES - low
            if 0 <= start < high - low:
                ready = mixed[head, :, start : start + LANES] / totals[head]
                piece = jnp.where(mine[:, start : start + LANES], ready, piece)
        pieces.append(piece.astype(jnp.bfloat16))
    attended = jnp.concatenate(pieces, axis=1)
    hidden = (
        tok_ref[...].astype(jnp.float32)
        + jnp.dot(attended, w_ref[...], preferred_element_type=jnp.float32)
    ).astype(jnp.bfloat16)
    owner_row = route_ref[0:1, :]
    owner_col = to_column(owner_row)
    down = lax.broadcasted_iota(jnp.int32, (rows, rows), 0)
    right = lax.broadcasted_iota(jnp.int32, (rows, rows), 1)
    earlier = (owner_col == owner_row) & (down < right // 4 * 4) & (down % 4 == 0)
    rank = jnp.sum(earlier.astype(jnp.int32), axis=0, keepdims=True)
    slot = 2 * owner_row + rank
    mrows = rows // 4
    merged = lax.broadcasted_iota(jnp.int32, (mrows, rows), 0)
    source = lax.broadcasted_iota(jnp.int32, (mrows, rows), 1)
    lane = lax.broadcasted_iota(jnp.int32, (mrows, LANES), 1)
    for quarter in range(4):
        pick = source == 4 * merged + quarter
        if quarter == 0:
            offset = jnp.sum(jnp.where(pick, route_ref[1:2, :], 0), axis=1, keepdims=True)
            code = jnp.sum(jnp.where(pick, slot, 0), axis=1, keepdims=True)
            tags = jnp.where(lane < LANES // 2, offset + 1, code + 1)
            out_ref[:, :LANES] = tags.astype(jnp.float32).astype(jnp.bfloat16)
        start = LANES + quarter * width
        out_ref[:, start : start + width] = jnp.dot(
            pick.astype(jnp.float32).astype(jnp.bfloat16), hidden, preferred_element_type=jnp.float32
        ).astype(jnp.bfloat16)
    for copy in started:
        copy.wait_send()


def to_row(column):
    size = column.shape[0]
    diagonal = lax.broadcasted_iota(jnp.int32, (size, size), 0) == lax.broadcasted_iota(
        jnp.int32, (size, size), 1
    )
    return jnp.sum(jnp.where(diagonal, column, 0.0), axis=0, keepdims=True)


def codes_of(tags):
    return to_row(tags.astype(jnp.float32)[:, LANES // 2 : LANES // 2 + 1])


def as_onehot(hit):
    return jnp.where(hit, 1.0, 0.0).astype(jnp.bfloat16)


def pick_rows(onehot, rows):
    return jnp.dot(onehot, rows, preferred_element_type=jnp.float32)


def route_kernel(
    nblk, r_ref, out_ref, near, comp, far, ordered, landed, nsend, nrecv, fsend, frecv, psend, precv
):
    me = lax.axis_index("blk")
    planes = nblk // PLANE
    plane, spot = lax.div(me, PLANE), lax.rem(me, PLANE)
    mrows, wide = r_ref.shape
    per = 2 * PLANE
    unit = (wide - LANES) // 20
    chunks = [(0, LANES + 5 * unit)]
    for share in (6, 6, 3):
        chunks.append((sum(chunks[-1]), share * unit))

    def along(distance):
        return lax.rem(plane + distance + planes, planes) * PLANE + spot

    def within(distance):
        return plane * PLANE + lax.rem(spot + distance, PLANE)

    barrier = pltpu.get_barrier_semaphore()
    peers = [along(d) for k in range(1, REACH + 1) for d in (k, -k)]
    peers += [within(d) for d in range(1, PLANE)]
    for other in peers:
        pl.semaphore_signal(barrier, inc=1, device_id={"blk": other}, device_id_type=pl.DeviceIdType.MESH)
    pl.semaphore_wait(barrier, len(peers))

    started = []

    def send(src, dst, sends, recvs, number, target):
        copy = pltpu.make_async_remote_copy(
            src_ref=src,
            dst_ref=dst,
            send_sem=sends.at[number],
            recv_sem=recvs.at[number],
            device_id={"blk": target},
            device_id_type=pl.DeviceIdType.MESH,
        )
        copy.start()
        started.append(copy)
        return copy

    def near_at(way, hop):
        return (way * REACH + hop - 1) * mrows

    def forward(way, hop, chunk):
        begin, size = chunks[chunk]
        cols = pl.ds(begin, size)
        src = r_ref.at[:, cols] if hop == 1 else near.at[pl.ds(near_at(way, hop - 1), mrows), cols]
        return send(
            src,
            near.at[pl.ds(near_at(way, hop), mrows), cols],
            nsend,
            nrecv,
            (way * REACH + hop - 1) * CHUNKS + chunk,
            along(1 - 2 * way),
        )

    hops = {}
    for chunk in range(CHUNKS):
        for way in range(2):
            hops[way, 1, chunk] = forward(way, 1, chunk)
    for hop in range(1, REACH):
        for chunk in range(CHUNKS):
            for way in range(2):
                hops[way, hop, chunk].wait_recv()
                hops[way, hop + 1, chunk] = forward(way, hop + 1, chunk)

    def far_at(way, ahead):
        return (way * (REACH - 1) + ahead - 1) * per if ahead < REACH else 2 * (REACH - 1) * per

    relays, onehots = {}, {}
    for chunk, (begin, size) in enumerate(chunks):
        for way in range(2):
            hops[way, REACH, chunk].wait_recv()
            held = near_at(way, REACH)
            if chunk == 0:
                code = codes_of(near[held : held + mrows, :LANES])
                index = lax.broadcasted_iota(jnp.int32, (REACH * per, mrows), 0)
                ahead = index // per + 1
                goal = plane + (ahead if way == 0 else planes - ahead)
                goal = jnp.where(goal >= planes, goal - planes, goal)
                want = goal * per + index % per + 1
                onehots[way] = as_onehot(code == want.astype(jnp.float32))
            comp[way * REACH * per : (way + 1) * REACH * per, begin : begin + size] = pick_rows(
                onehots[way], near[held : held + mrows, begin : begin + size]
            ).astype(jnp.bfloat16)
            for ahead in range(REACH, 0, -1):
                if ahead == REACH and chunk * 2 // CHUNKS != way:
                    continue
                relays[way, ahead, chunk] = send(
                    comp.at[pl.ds((way * REACH + ahead - 1) * per, per), pl.ds(begin, size)],
                    far.at[pl.ds(far_at(way, ahead), per), pl.ds(begin, size)],
                    fsend,
                    frecv,
                    (way * REACH + ahead - 1) * CHUNKS + chunk,
                    along(ahead - 2 * way * ahead),
                )

    slots = per * planes
    each = slots // PLANE

    def wanted(columns):
        index = lax.broadcasted_iota(jnp.int32, (slots, columns), 0)
        column = lax.broadcasted_iota(jnp.int32, (slots, columns), 1)
        return index % each // 2, index // each * 2 + index % 2, column

    base = plane * per + 1
    group, local, column = wanted(mrows)
    code = codes_of(r_ref[:, :LANES])
    own_hot = as_onehot((group == 0) & (code == (local + base).astype(jnp.float32)))
    group, local, column = wanted(2 * REACH * mrows)
    code = codes_of(near[:, :LANES])
    near_hot = as_onehot(
        (group == 1 + column // mrows) & (code == (local + base).astype(jnp.float32))
    )
    group, local, column = wanted(far.shape[0])
    far_hot = as_onehot((group == 1 + 2 * REACH + column // per) & (local == column % per))

    spread = {}
    mine = pl.ds(pl.multiple_of(spot * each, each), each)
    for chunk, (begin, size) in enumerate(chunks):
        cols = slice(begin, begin + size)
        found = pick_rows(own_hot, r_ref[:, cols]) + pick_rows(near_hot, near[:, cols])
        for way in range(2):
            for ahead in range(1, REACH + 1):
                if (way, ahead, chunk) in relays:
                    relays[way, ahead, chunk].wait_recv()
        ordered[:, cols] = (found + pick_rows(far_hot, far[:, cols])).astype(jnp.bfloat16)
        for distance in range(1, PLANE):
            theirs = pl.ds(pl.multiple_of(lax.rem(spot + distance, PLANE) * each, each), each)
            spread[distance, chunk] = send(
                ordered.at[theirs, pl.ds(begin, size)],
                landed.at[mine, pl.ds(begin, size)],
                psend,
                precv,
                (distance - 1) * CHUNKS + chunk,
                within(distance),
            )
        landed[mine, cols] = ordered[mine, cols]

    for chunk, (begin, size) in enumerate(chunks):
        for distance in range(1, PLANE):
            spread[distance, chunk].wait_recv()
        if chunk == 0:
            tag = to_row(landed[:, :LANES].astype(jnp.float32)[:, 0:1])
            index = lax.broadcasted_iota(jnp.int32, (out_ref.shape[0], slots), 0) + 1
            place = as_onehot(index.astype(jnp.float32) == tag)
            begin, size = begin + LANES, size - LANES
        out_ref[:, begin - LANES : begin - LANES + size] = pick_rows(
            place, landed[:, begin : begin + size]
        ).astype(jnp.bfloat16)
    for copy in started:
        copy.wait_send()


def route_rows(rows, nblk, capacity):
    mrows, wide = rows.shape
    per = 2 * PLANE
    vmem = pl.BlockSpec(memory_space=pltpu.VMEM)
    dma = pltpu.SemaphoreType.DMA
    return pl.pallas_call(
        functools.partial(route_kernel, nblk),
        out_shape=jax.ShapeDtypeStruct((capacity, wide - LANES), rows.dtype),
        in_specs=[vmem],
        out_specs=vmem,
        scratch_shapes=[
            pltpu.VMEM((2 * REACH * mrows, wide), rows.dtype),
            pltpu.VMEM((2 * REACH * per, wide), rows.dtype),
            pltpu.VMEM(((2 * REACH - 1) * per, wide), rows.dtype),
            pltpu.VMEM((2 * nblk, wide), rows.dtype),
            pltpu.VMEM((2 * nblk, wide), rows.dtype),
        ]
        + [dma((2 * REACH * CHUNKS,))] * 4
        + [dma(((PLANE - 1) * CHUNKS,))] * 2,
        compiler_params=pltpu.CompilerParams(
            collective_id=1, has_side_effects=True, vmem_limit_bytes=48 * 2**20
        ),
    )(rows)


def per_device(segment_ids, block_mask, queries, keys, values, tokens, out_weight, owners, offsets):
    rows = queries.shape[0]
    width = tokens.shape[1]
    nblk = lax.axis_size("blk")
    mrows = rows // 4
    capacity = 2 * mrows
    wide = 4 * width + LANES
    route = jnp.broadcast_to(jnp.stack([owners, offsets])[:, :, None], (2, mrows, 4)).reshape(2, rows)
    operands = (
        queries,
        keys,
        values,
        segment_ids.reshape(nblk, rows),
        block_mask,
        tokens,
        out_weight,
        route,
    )
    halo = pltpu.VMEM((2 * SPAN,) + keys.shape, keys.dtype)
    dma = pltpu.SemaphoreType.DMA
    outgoing = pl.pallas_call(
        attend_kernel,
        out_shape=jax.ShapeDtypeStruct((mrows, wide), jnp.bfloat16),
        in_specs=[pl.BlockSpec(memory_space=pl.ANY)] * len(operands),
        out_specs=pl.BlockSpec(memory_space=pltpu.VMEM),
        scratch_shapes=[pltpu.VMEM(x.shape, x.dtype) for x in operands]
        + [
            halo,
            halo,
            pltpu.VMEM((HEADS, rows, 1), jnp.float32),
            pltpu.VMEM((HEADS, rows, 1), jnp.float32),
            pltpu.VMEM((HEADS, rows, 2 * LANES), jnp.float32),
            dma((len(operands),)),
        ]
        + [dma((2 * SPAN * PARTS,))] * 4,
        compiler_params=pltpu.CompilerParams(
            collective_id=0, has_side_effects=True, vmem_limit_bytes=56 * 2**20
        ),
    )(*operands)
    return route_rows(outgoing, nblk, capacity)


def solution(mesh):
    placed = (
        P("rep"),
        P("rep", None),
        P(("rep", "blk"), None),
        P(("rep", "blk"), None),
        P(("rep", "blk"), None),
        P(("rep", "blk"), None),
        P(),
        P(("rep", "blk")),
        P(("rep", "blk")),
    )
    return jax.shard_map(
        per_device, mesh=mesh, in_specs=placed, out_specs=P(("rep", "blk"), None), check_vma=False
    )
```

```python
import functools

import jax
import jax.numpy as jnp
from jax import lax
from jax.experimental import pallas as pl
from jax.experimental.pallas import tpu as pltpu
from jax.sharding import PartitionSpec as P

HEADS = 8
SPAN = 3
NEG = -1e30
LANES = 128
PLANE = 8
REACH = 4
CHUNKS = 4
PARTS = 2


def to_column(row):
    size = row.shape[1]
    diagonal = lax.broadcasted_iota(jnp.int32, (size, size), 0) == lax.broadcasted_iota(
        jnp.int32, (size, size), 1
    )
    return jnp.sum(jnp.where(diagonal, row, 0), axis=1, keepdims=True)


def to_row(column):
    size = column.shape[0]
    diagonal = lax.broadcasted_iota(jnp.int32, (size, size), 0) == lax.broadcasted_iota(
        jnp.int32, (size, size), 1
    )
    return jnp.sum(jnp.where(diagonal, column, 0.0), axis=0, keepdims=True)


def codes_of(tags):
    return to_row(tags.astype(jnp.float32)[:, LANES // 2 : LANES // 2 + 1])


def as_onehot(hit):
    return jnp.where(hit, 1.0, 0.0).astype(jnp.bfloat16)


def pick_rows(onehot, rows):
    return jnp.dot(onehot, rows, preferred_element_type=jnp.float32)


def program_kernel(
    q_hbm, k_hbm, v_hbm, seg_hbm, mask_hbm, tok_hbm, w_hbm, owner_hbm, offset_hbm, out_ref,
    q_ref, k_ref, v_ref, seg_ref, mask_ref, tok_ref, w_ref, owner_ref, offset_ref,
    kh, vh, peaks, totals, mixed, r_ref, near, comp, far_rows, ordered, landed,
    loads, ksend, vsend, krecv, vrecv, nsend, nrecv, fsend, frecv, psend, precv,
):
    rows, features = q_ref.shape
    nblk = mask_ref.shape[0]
    width = tok_ref.shape[1]
    hdim = features // HEADS
    block = lax.axis_index("blk")
    scale = 1.0 / jnp.sqrt(jnp.float32(hdim))

    pairs = [
        (q_hbm, q_ref),
        (k_hbm, k_ref),
        (v_hbm, v_ref),
        (seg_hbm, seg_ref),
        (mask_hbm, mask_ref),
        (owner_hbm, owner_ref),
        (offset_hbm, offset_ref),
        (tok_hbm, tok_ref),
        (w_hbm, w_ref),
    ]
    local = [pltpu.make_async_copy(src, dst, loads.at[n]) for n, (src, dst) in enumerate(pairs)]
    for copy in local:
        copy.start()

    rungs = nblk // 2
    rung, side = lax.div(block, 2), lax.rem(block, 2)
    up = lax.rem(rung + 1, rungs) * 2 + side
    down = lax.rem(rung + rungs - 1, rungs) * 2 + side
    across = rung * 2 + 1 - side
    far = lax.rem(rung + 1 - 2 * side + rungs, rungs) * 2 + side
    back = lax.rem(rung - 1 + 2 * side + rungs, rungs) * 2 + side

    planes = nblk // PLANE
    plane, spot = lax.div(block, PLANE), lax.rem(block, PLANE)

    def along(distance):
        return lax.rem(plane + distance + planes, planes) * PLANE + spot

    def within(distance):
        return plane * PLANE + lax.rem(spot + distance, PLANE)

    barrier = pltpu.get_barrier_semaphore()
    peers = [up, down, across]
    peers += [along(d) for k in range(1, REACH + 1) for d in (k, -k)]
    peers += [within(d) for d in range(1, PLANE)]
    for other in peers:
        pl.semaphore_signal(barrier, inc=1, device_id={"blk": other}, device_id_type=pl.DeviceIdType.MESH)
    pl.semaphore_wait(barrier, len(peers))

    half = rows // PARTS
    started = []

    def send(src, dst, sends, recvs, number, slot, part, target):
        span = pl.ds(part * half, half)
        copy = pltpu.make_async_remote_copy(
            src_ref=src.at[span],
            dst_ref=dst.at[slot, span],
            send_sem=sends.at[number * PARTS + part],
            recv_sem=recvs.at[slot * PARTS + part],
            device_id={"blk": target},
            device_id_type=pl.DeviceIdType.MESH,
        )
        copy.start()
        started.append(copy)

    def arrived(dst, recvs, slot, part):
        span = pl.ds(part * half, half)
        pltpu.make_async_copy(
            dst.at[slot, span], dst.at[slot, span], recvs.at[slot * PARTS + part]
        ).wait()

    for part in range(PARTS):
        send(v_hbm, vh, vsend, vrecv, 0, 2 + side, part, across)
        send(k_hbm, kh, ksend, krecv, 1, 4 - 3 * side, part, back)
        send(k_hbm, kh, ksend, krecv, 2, 1 + 3 * side, part, far)
    for part in range(PARTS):
        send(k_hbm, kh, ksend, krecv, 0, 2 + side, part, across)
        send(v_hbm, vh, vsend, vrecv, 2, 1 + 3 * side, part, far)
        send(v_hbm, vh, vsend, vrecv, 1, 4 - 3 * side, part, back)
    for part in range(PARTS):
        arrived(vh, vrecv, 3 - side, part)
        send(vh.at[3 - side], vh, vsend, vrecv, 3, 2 + side, part, far)
        send(vh.at[3 - side], vh, vsend, vrecv, 4, 5 - 5 * side, part, back)
    for part in range(PARTS):
        arrived(kh, krecv, 4 - 3 * side, part)
        send(kh.at[4 - 3 * side], kh, ksend, krecv, 3, 3 - side, part, across)
    for part in range(PARTS):
        arrived(kh, krecv, 1 + 3 * side, part)
        send(kh.at[1 + 3 * side], kh, ksend, krecv, 4, 5 * side, part, across)

    for copy in local:
        copy.wait()

    def ids_of(column):
        halves = rows // LANES
        return jnp.concatenate(
            [seg_ref[pl.ds(column * halves + n, 1), :] for n in range(halves)], axis=1
        )

    query_seg = to_column(ids_of(block))
    mask_row = mask_ref[pl.ds(block, 1), :]
    columns = lax.broadcasted_iota(jnp.int32, mask_row.shape, 1)

    def segments(dist):
        column = block + dist
        flag = jnp.sum(jnp.where(columns == column, mask_row, 0), axis=1, keepdims=True)
        return jnp.where(flag > 0, ids_of(lax.rem(column + nblk, nblk)), -1)

    def window(head):
        first, last = head * hdim, (head + 1) * hdim
        low, high = first // LANES * LANES, -(-last // LANES) * LANES
        lane = lax.broadcasted_iota(jnp.int32, (rows, high - low), 1) + low
        return low, high, (lane >= first) & (lane < last)

    def attend(blocks, fresh):
        for head in range(HEADS):
            low, high, mine = window(head)
            query = jnp.where(mine, q_ref[:, low:high], jnp.bfloat16(0))
            scores = []
            for key, _, key_seg in blocks:
                part = lax.dot_general(
                    query,
                    key[:, low:high],
                    (((1,), (1,)), ((), ())),
                    preferred_element_type=jnp.float32,
                )
                scores.append(jnp.where(query_seg == key_seg, part, NEG))
            peak = jnp.max(functools.reduce(jnp.maximum, scores), axis=1, keepdims=True)
            if fresh:
                total = jnp.zeros((rows, 1), jnp.float32)
                result = jnp.zeros((rows, high - low), jnp.float32)
            else:
                before = peaks[head]
                peak = jnp.maximum(peak, before)
                factor = jnp.exp((before - peak) * scale)
                total = totals[head] * factor
                result = mixed[head, :, : high - low] * factor
            for (_, value, _), part in zip(blocks, scores):
                weights = jnp.exp((part - peak) * scale)
                total = total + jnp.sum(weights, axis=1, keepdims=True)
                result = result + jnp.dot(
                    weights.astype(jnp.bfloat16), value[:, low:high], preferred_element_type=jnp.float32
                )
            peaks[head] = peak
            totals[head] = total
            mixed[head, :, : high - low] = result

    def held(slot, dist):
        return kh.at[slot], vh.at[slot], segments(dist)

    for part in range(PARTS):
        arrived(kh, krecv, 3 - side, part)
        arrived(vh, vrecv, 1, part)
        arrived(vh, vrecv, 4, part)
    attend(
        [(k_ref, v_ref, segments(0)), held(3 - side, 1 - 2 * side), held(1, -2), held(4, 2)], True
    )
    for part in range(PARTS):
        arrived(vh, vrecv, 2 + side, part)
        send(vh.at[2 + side], vh, vsend, vrecv, 5, 5 * side, part, far)
    for part in range(PARTS):
        arrived(kh, krecv, 2 + side, part)
        send(kh.at[2 + side], kh, ksend, krecv, 5, 5 * side, part, far)
    for part in range(PARTS):
        arrived(vh, vrecv, 5 - 5 * side, part)
        arrived(kh, krecv, 5 - 5 * side, part)
    attend([held(2 + side, 2 * side - 1), held(5 - 5 * side, 3 - 6 * side)], False)
    owner_row = owner_ref[...]
    mrows, wide = r_ref.shape
    earlier = (to_column(owner_row) == owner_row) & (
        lax.broadcasted_iota(jnp.int32, (mrows, mrows), 0)
        < lax.broadcasted_iota(jnp.int32, (mrows, mrows), 1)
    )
    rank = jnp.sum(earlier.astype(jnp.int32), axis=0, keepdims=True)
    lane = lax.broadcasted_iota(jnp.int32, (mrows, LANES), 1)
    offset, code = to_column(offset_ref[...]), to_column(2 * owner_row + rank)
    tags = jnp.where(lane < LANES // 2, offset + 1, code + 1)
    r_ref[:, :LANES] = tags.astype(jnp.float32).astype(jnp.bfloat16)
    for part in range(PARTS):
        arrived(vh, vrecv, 5 * side, part)
        arrived(kh, krecv, 5 * side, part)
    attend([held(5 * side, 6 * side - 3)], False)

    pieces = []
    for group in range(features // LANES):
        piece = jnp.zeros((rows, LANES), jnp.float32)
        for head in range(HEADS):
            low, high, mine = window(head)
            start = group * LANES - low
            if 0 <= start < high - low:
                ready = mixed[head, :, start : start + LANES] / totals[head]
                piece = jnp.where(mine[:, start : start + LANES], ready, piece)
        pieces.append(piece.astype(jnp.bfloat16))
    attended = jnp.concatenate(pieces, axis=1)
    hidden = (
        tok_ref[...].astype(jnp.float32)
        + jnp.dot(attended, w_ref[...], preferred_element_type=jnp.float32)
    ).astype(jnp.bfloat16)
    merged = lax.broadcasted_iota(jnp.int32, (mrows, rows), 0)
    source = lax.broadcasted_iota(jnp.int32, (mrows, rows), 1)
    per = 2 * PLANE
    unit = (wide - LANES) // 20
    chunks = [(0, LANES + 5 * unit)]
    for share in (6, 6, 3):
        chunks.append((sum(chunks[-1]), share * unit))

    def pass_on(src, dst, sends, recvs, number, target):
        copy = pltpu.make_async_remote_copy(
            src_ref=src,
            dst_ref=dst,
            send_sem=sends.at[number],
            recv_sem=recvs.at[number],
            device_id={"blk": target},
            device_id_type=pl.DeviceIdType.MESH,
        )
        copy.start()
        started.append(copy)
        return copy

    def near_at(way, hop):
        return (way * REACH + hop - 1) * mrows

    def forward(way, hop, chunk):
        begin, size = chunks[chunk]
        cols = pl.ds(begin, size)
        src = r_ref.at[:, cols] if hop == 1 else near.at[pl.ds(near_at(way, hop - 1), mrows), cols]
        return pass_on(
            src,
            near.at[pl.ds(near_at(way, hop), mrows), cols],
            nsend,
            nrecv,
            (way * REACH + hop - 1) * CHUNKS + chunk,
            along(1 - 2 * way),
        )

    hops = {}
    built = 0
    for quarter in range(4):
        pick = source == 4 * merged + quarter
        built = LANES + (quarter + 1) * width
        r_ref[:, built - width : built] = pick_rows(as_onehot(pick), hidden).astype(jnp.bfloat16)
        for chunk, (begin, size) in enumerate(chunks):
            if built - width < begin + size <= built:
                for way in range(2):
                    hops[way, 1, chunk] = forward(way, 1, chunk)
    for hop in range(1, REACH):
        for chunk in range(CHUNKS):
            for way in range(2):
                hops[way, hop, chunk].wait_recv()
                hops[way, hop + 1, chunk] = forward(way, hop + 1, chunk)

    def far_at(way, ahead):
        return (way * (REACH - 1) + ahead - 1) * per if ahead < REACH else 2 * (REACH - 1) * per

    relays, onehots = {}, {}
    for chunk, (begin, size) in enumerate(chunks):
        for way in range(2):
            hops[way, REACH, chunk].wait_recv()
            held = near_at(way, REACH)
            if chunk == 0:
                code = codes_of(near[held : held + mrows, :LANES])
                index = lax.broadcasted_iota(jnp.int32, (REACH * per, mrows), 0)
                ahead = index // per + 1
                goal = plane + (ahead if way == 0 else planes - ahead)
                goal = jnp.where(goal >= planes, goal - planes, goal)
                want = goal * per + index % per + 1
                onehots[way] = as_onehot(code == want.astype(jnp.float32))
            comp[way * REACH * per : (way + 1) * REACH * per, begin : begin + size] = pick_rows(
                onehots[way], near[held : held + mrows, begin : begin + size]
            ).astype(jnp.bfloat16)
            for ahead in range(REACH, 0, -1):
                if ahead == REACH and chunk * 2 // CHUNKS != way:
                    continue
                relays[way, ahead, chunk] = pass_on(
                    comp.at[pl.ds((way * REACH + ahead - 1) * per, per), pl.ds(begin, size)],
                    far_rows.at[pl.ds(far_at(way, ahead), per), pl.ds(begin, size)],
                    fsend,
                    frecv,
                    (way * REACH + ahead - 1) * CHUNKS + chunk,
                    along(ahead - 2 * way * ahead),
                )

    slots = per * planes
    each = slots // PLANE

    def wanted(columns):
        index = lax.broadcasted_iota(jnp.int32, (slots, columns), 0)
        column = lax.broadcasted_iota(jnp.int32, (slots, columns), 1)
        return index % each // 2, index // each * 2 + index % 2, column

    base = plane * per + 1
    group, local, column = wanted(mrows)
    code = codes_of(r_ref[:, :LANES])
    own_hot = as_onehot((group == 0) & (code == (local + base).astype(jnp.float32)))
    group, local, column = wanted(2 * REACH * mrows)
    code = codes_of(near[:, :LANES])
    near_hot = as_onehot(
        (group == 1 + column // mrows) & (code == (local + base).astype(jnp.float32))
    )
    group, local, column = wanted(far_rows.shape[0])
    far_hot = as_onehot((group == 1 + 2 * REACH + column // per) & (local == column % per))

    spread = {}
    mine = pl.ds(pl.multiple_of(spot * each, each), each)
    for chunk, (begin, size) in enumerate(chunks):
        cols = slice(begin, begin + size)
        found = pick_rows(own_hot, r_ref[:, cols]) + pick_rows(near_hot, near[:, cols])
        for way in range(2):
            for ahead in range(1, REACH + 1):
                if (way, ahead, chunk) in relays:
                    relays[way, ahead, chunk].wait_recv()
        ordered[:, cols] = (found + pick_rows(far_hot, far_rows[:, cols])).astype(jnp.bfloat16)
        for distance in range(1, PLANE):
            theirs = pl.ds(pl.multiple_of(lax.rem(spot + distance, PLANE) * each, each), each)
            spread[distance, chunk] = pass_on(
                ordered.at[theirs, pl.ds(begin, size)],
                landed.at[mine, pl.ds(begin, size)],
                psend,
                precv,
                (distance - 1) * CHUNKS + chunk,
                within(distance),
            )
        landed[mine, cols] = ordered[mine, cols]

    for chunk, (begin, size) in enumerate(chunks):
        for distance in range(1, PLANE):
            spread[distance, chunk].wait_recv()
        if chunk == 0:
            tag = to_row(landed[:, :LANES].astype(jnp.float32)[:, 0:1])
            index = lax.broadcasted_iota(jnp.int32, (out_ref.shape[0], slots), 0) + 1
            place = as_onehot(index.astype(jnp.float32) == tag)
            begin, size = begin + LANES, size - LANES
        out_ref[:, begin - LANES : begin - LANES + size] = pick_rows(
            place, landed[:, begin : begin + size]
        ).astype(jnp.bfloat16)
    for copy in started:
        copy.wait_send()


def per_device(segment_ids, block_mask, queries, keys, values, tokens, out_weight, owners, offsets):
    rows = queries.shape[0]
    width = tokens.shape[1]
    nblk = lax.axis_size("blk")
    mrows = rows // 4
    capacity = 2 * mrows
    wide = 4 * width + LANES
    per = 2 * PLANE
    operands = (
        queries,
        keys,
        values,
        segment_ids.reshape(-1, LANES),
        block_mask,
        tokens,
        out_weight,
        owners.reshape(1, mrows),
        offsets.reshape(1, mrows),
    )
    halo = pltpu.VMEM((2 * SPAN,) + keys.shape, keys.dtype)
    dma = pltpu.SemaphoreType.DMA

    def held(count):
        return pltpu.VMEM((count, wide), tokens.dtype)

    return pl.pallas_call(
        program_kernel,
        out_shape=jax.ShapeDtypeStruct((capacity, 4 * width), tokens.dtype),
        in_specs=[pl.BlockSpec(memory_space=pl.ANY)] * len(operands),
        out_specs=pl.BlockSpec(memory_space=pltpu.VMEM),
        scratch_shapes=[pltpu.VMEM(x.shape, x.dtype) for x in operands]
        + [
            halo,
            halo,
            pltpu.VMEM((HEADS, rows, 1), jnp.float32),
            pltpu.VMEM((HEADS, rows, 1), jnp.float32),
            pltpu.VMEM((HEADS, rows, 2 * LANES), jnp.float32),
            held(mrows),
            held(2 * REACH * mrows),
            held(2 * REACH * per),
            held((2 * REACH - 1) * per),
            held(2 * nblk),
            held(2 * nblk),
            dma((len(operands),)),
        ]
        + [dma((2 * SPAN * PARTS,))] * 4
        + [dma((2 * REACH * CHUNKS,))] * 4
        + [dma(((PLANE - 1) * CHUNKS,))] * 2,
        compiler_params=pltpu.CompilerParams(
            collective_id=0, has_side_effects=True, vmem_limit_bytes=56 * 2**20
        ),
    )(*operands)


def solution(mesh):
    placed = (
        P("rep"),
        P("rep", None),
        P(("rep", "blk"), None),
        P(("rep", "blk"), None),
        P(("rep", "blk"), None),
        P(("rep", "blk"), None),
        P(),
        P(("rep", "blk")),
        P(("rep", "blk")),
    )
    return jax.shard_map(
        per_device, mesh=mesh, in_specs=placed, out_specs=P(("rep", "blk"), None), check_vma=False
    )
```

```python
import functools

import jax
import jax.numpy as jnp
from jax import lax
from jax.experimental import pallas as pl
from jax.experimental.pallas import tpu as pltpu
from jax.sharding import PartitionSpec as P

HEADS = 8
SPAN = 3
NEG = -1e30
LANES = 128
PLANE = 8
REACH = 4
CHUNKS = 4
PARTS = 2


def to_column(row):
    size = row.shape[1]
    diagonal = lax.broadcasted_iota(jnp.int32, (size, size), 0) == lax.broadcasted_iota(
        jnp.int32, (size, size), 1
    )
    return jnp.sum(jnp.where(diagonal, row, 0), axis=1, keepdims=True)


def to_row(column):
    size = column.shape[0]
    diagonal = lax.broadcasted_iota(jnp.int32, (size, size), 0) == lax.broadcasted_iota(
        jnp.int32, (size, size), 1
    )
    return jnp.sum(jnp.where(diagonal, column, 0.0), axis=0, keepdims=True)


def codes_of(tags):
    return to_row(tags.astype(jnp.float32)[:, LANES // 2 : LANES // 2 + 1])


def as_onehot(hit):
    return jnp.where(hit, 1.0, 0.0).astype(jnp.bfloat16)


def pick_rows(onehot, rows):
    return jnp.dot(onehot, rows, preferred_element_type=jnp.float32)


def program_kernel(
    q_hbm, k_hbm, v_hbm, seg_hbm, mask_hbm, tok_hbm, w_hbm, owner_hbm, offset_hbm, out_ref,
    q_ref, k_ref, v_ref, seg_ref, mask_ref, tok_ref, w_ref, owner_ref, offset_ref,
    kh, vh, peaks, totals, mixed, r_ref, near, comp, far_rows, ordered, landed,
    loads, ksend, vsend, krecv, vrecv, nsend, nrecv, fsend, frecv, psend, precv,
):
    rows, features = q_ref.shape
    nblk = mask_ref.shape[0]
    width = tok_ref.shape[1]
    hdim = features // HEADS
    block = lax.axis_index("blk")
    scale = 1.0 / jnp.sqrt(jnp.float32(hdim))

    pairs = [
        (q_hbm, q_ref),
        (k_hbm, k_ref),
        (v_hbm, v_ref),
        (seg_hbm, seg_ref),
        (mask_hbm, mask_ref),
        (owner_hbm, owner_ref),
        (offset_hbm, offset_ref),
        (tok_hbm, tok_ref),
        (w_hbm, w_ref),
    ]
    local = [pltpu.make_async_copy(src, dst, loads.at[n]) for n, (src, dst) in enumerate(pairs)]
    for copy in local:
        copy.start()

    rungs = nblk // 2
    rung, side = lax.div(block, 2), lax.rem(block, 2)
    up = lax.rem(rung + 1, rungs) * 2 + side
    down = lax.rem(rung + rungs - 1, rungs) * 2 + side
    across = rung * 2 + 1 - side
    far = lax.rem(rung + 1 - 2 * side + rungs, rungs) * 2 + side
    back = lax.rem(rung - 1 + 2 * side + rungs, rungs) * 2 + side

    planes = nblk // PLANE
    plane, spot = lax.div(block, PLANE), lax.rem(block, PLANE)

    def along(distance):
        return lax.rem(plane + distance + planes, planes) * PLANE + spot

    def within(distance):
        return plane * PLANE + lax.rem(spot + distance, PLANE)

    barrier = pltpu.get_barrier_semaphore()
    peers = [up, down, across]
    peers += [along(d) for k in range(1, REACH + 1) for d in (k, -k)]
    peers += [within(d) for d in range(1, PLANE)]
    for other in peers:
        pl.semaphore_signal(barrier, inc=1, device_id={"blk": other}, device_id_type=pl.DeviceIdType.MESH)
    pl.semaphore_wait(barrier, len(peers))

    half = rows // PARTS
    started = []

    def send(src, dst, sends, recvs, number, slot, part, target):
        span = pl.ds(part * half, half)
        copy = pltpu.make_async_remote_copy(
            src_ref=src.at[span],
            dst_ref=dst.at[slot, span],
            send_sem=sends.at[number * PARTS + part],
            recv_sem=recvs.at[slot * PARTS + part],
            device_id={"blk": target},
            device_id_type=pl.DeviceIdType.MESH,
        )
        copy.start()
        started.append(copy)

    def arrived(dst, recvs, slot, part):
        span = pl.ds(part * half, half)
        pltpu.make_async_copy(
            dst.at[slot, span], dst.at[slot, span], recvs.at[slot * PARTS + part]
        ).wait()

    for part in range(PARTS):
        send(v_hbm, vh, vsend, vrecv, 0, 2 + side, part, across)
        send(k_hbm, kh, ksend, krecv, 1, 4 - 3 * side, part, back)
        send(k_hbm, kh, ksend, krecv, 2, 1 + 3 * side, part, far)
    for part in range(PARTS):
        send(k_hbm, kh, ksend, krecv, 0, 2 + side, part, across)
        send(v_hbm, vh, vsend, vrecv, 2, 1 + 3 * side, part, far)
        send(v_hbm, vh, vsend, vrecv, 1, 4 - 3 * side, part, back)
    for copy in local:
        copy.wait()

    def ids_of(column):
        halves = rows // LANES
        return jnp.concatenate(
            [seg_ref[pl.ds(column * halves + n, 1), :] for n in range(halves)], axis=1
        )

    query_seg = to_column(ids_of(block))
    mask_row = mask_ref[pl.ds(block, 1), :]
    columns = lax.broadcasted_iota(jnp.int32, mask_row.shape, 1)

    def segments(dist):
        column = block + dist
        flag = jnp.sum(jnp.where(columns == column, mask_row, 0), axis=1, keepdims=True)
        return jnp.where(flag > 0, ids_of(lax.rem(column + nblk, nblk)), -1)

    def window(head):
        first, last = head * hdim, (head + 1) * hdim
        low, high = first // LANES * LANES, -(-last // LANES) * LANES
        lane = lax.broadcasted_iota(jnp.int32, (rows, high - low), 1) + low
        return low, high, (lane >= first) & (lane < last)

    def attend(blocks, fresh):
        for head in range(HEADS):
            low, high, mine = window(head)
            query = jnp.where(mine, q_ref[:, low:high], jnp.bfloat16(0))
            scores = []
            for key, _, key_seg in blocks:
                part = lax.dot_general(
                    query,
                    key[:, low:high],
                    (((1,), (1,)), ((), ())),
                    preferred_element_type=jnp.float32,
                )
                scores.append(jnp.where(query_seg == key_seg, part, NEG))
            peak = jnp.max(functools.reduce(jnp.maximum, scores), axis=1, keepdims=True)
            if fresh:
                total = jnp.zeros((rows, 1), jnp.float32)
                result = jnp.zeros((rows, high - low), jnp.float32)
            else:
                before = peaks[head]
                peak = jnp.maximum(peak, before)
                factor = jnp.exp((before - peak) * scale)
                total = totals[head] * factor
                result = mixed[head, :, : high - low] * factor
            for (_, value, _), part in zip(blocks, scores):
                weights = jnp.exp((part - peak) * scale)
                total = total + jnp.sum(weights, axis=1, keepdims=True)
                result = result + jnp.dot(
                    weights.astype(jnp.bfloat16), value[:, low:high], preferred_element_type=jnp.float32
                )
            peaks[head] = peak
            totals[head] = total
            mixed[head, :, : high - low] = result

    def held(slot, dist):
        return kh.at[slot], vh.at[slot], segments(dist)

    attend([(k_ref, v_ref, segments(0))], True)
    for part in range(PARTS):
        arrived(vh, vrecv, 3 - side, part)
        send(vh.at[3 - side], vh, vsend, vrecv, 3, 2 + side, part, far)
        send(vh.at[3 - side], vh, vsend, vrecv, 4, 5 - 5 * side, part, back)
    for part in range(PARTS):
        arrived(kh, krecv, 4 - 3 * side, part)
        send(kh.at[4 - 3 * side], kh, ksend, krecv, 3, 3 - side, part, across)
    for part in range(PARTS):
        arrived(kh, krecv, 1 + 3 * side, part)
        send(kh.at[1 + 3 * side], kh, ksend, krecv, 4, 5 * side, part, across)

    for part in range(PARTS):
        arrived(kh, krecv, 3 - side, part)
    attend([held(3 - side, 1 - 2 * side)], False)
    for part in range(PARTS):
        arrived(vh, vrecv, 2 + side, part)
        send(vh.at[2 + side], vh, vsend, vrecv, 5, 5 * side, part, far)
    for part in range(PARTS):
        arrived(kh, krecv, 2 + side, part)
        send(kh.at[2 + side], kh, ksend, krecv, 5, 5 * side, part, far)
    for part in range(PARTS):
        arrived(vh, vrecv, 1, part)
        arrived(vh, vrecv, 4, part)
    attend([held(1, -2), held(4, 2)], False)
    for part in range(PARTS):
        arrived(vh, vrecv, 5 - 5 * side, part)
        arrived(kh, krecv, 5 - 5 * side, part)
    attend([held(2 + side, 2 * side - 1), held(5 - 5 * side, 3 - 6 * side)], False)
    owner_row = owner_ref[...]
    mrows, wide = r_ref.shape
    earlier = (to_column(owner_row) == owner_row) & (
        lax.broadcasted_iota(jnp.int32, (mrows, mrows), 0)
        < lax.broadcasted_iota(jnp.int32, (mrows, mrows), 1)
    )
    rank = jnp.sum(earlier.astype(jnp.int32), axis=0, keepdims=True)
    lane = lax.broadcasted_iota(jnp.int32, (mrows, LANES), 1)
    offset, code = to_column(offset_ref[...]), to_column(2 * owner_row + rank)
    tags = jnp.where(lane < LANES // 2, offset + 1, code + 1)
    r_ref[:, :LANES] = tags.astype(jnp.float32).astype(jnp.bfloat16)
    for part in range(PARTS):
        arrived(vh, vrecv, 5 * side, part)
        arrived(kh, krecv, 5 * side, part)
    attend([held(5 * side, 6 * side - 3)], False)

    pieces = []
    for group in range(features // LANES):
        piece = jnp.zeros((rows, LANES), jnp.float32)
        for head in range(HEADS):
            low, high, mine = window(head)
            start = group * LANES - low
            if 0 <= start < high - low:
                ready = mixed[head, :, start : start + LANES] / totals[head]
                piece = jnp.where(mine[:, start : start + LANES], ready, piece)
        pieces.append(piece.astype(jnp.bfloat16))
    attended = jnp.concatenate(pieces, axis=1)
    hidden = (
        tok_ref[...].astype(jnp.float32)
        + jnp.dot(attended, w_ref[...], preferred_element_type=jnp.float32)
    ).astype(jnp.bfloat16)
    merged = lax.broadcasted_iota(jnp.int32, (mrows, rows), 0)
    source = lax.broadcasted_iota(jnp.int32, (mrows, rows), 1)
    per = 2 * PLANE
    unit = (wide - LANES) // 20
    chunks = [(0, LANES + 5 * unit)]
    for share in (7, 6, 2):
        chunks.append((sum(chunks[-1]), share * unit))

    def pass_on(src, dst, sends, recvs, number, target):
        copy = pltpu.make_async_remote_copy(
            src_ref=src,
            dst_ref=dst,
            send_sem=sends.at[number],
            recv_sem=recvs.at[number],
            device_id={"blk": target},
            device_id_type=pl.DeviceIdType.MESH,
        )
        copy.start()
        started.append(copy)
        return copy

    def near_at(way, hop):
        return (way * REACH + hop - 1) * mrows

    def forward(way, hop, chunk):
        begin, size = chunks[chunk]
        cols = pl.ds(begin, size)
        src = r_ref.at[:, cols] if hop == 1 else near.at[pl.ds(near_at(way, hop - 1), mrows), cols]
        return pass_on(
            src,
            near.at[pl.ds(near_at(way, hop), mrows), cols],
            nsend,
            nrecv,
            (way * REACH + hop - 1) * CHUNKS + chunk,
            along(1 - 2 * way),
        )

    hops = {}
    built = 0
    for quarter in range(4):
        pick = source == 4 * merged + quarter
        built = LANES + (quarter + 1) * width
        r_ref[:, built - width : built] = pick_rows(as_onehot(pick), hidden).astype(jnp.bfloat16)
        for chunk, (begin, size) in enumerate(chunks):
            if built - width < begin + size <= built:
                for way in range(2):
                    hops[way, 1, chunk] = forward(way, 1, chunk)
    for hop in range(1, REACH):
        for chunk in range(CHUNKS):
            for way in range(2):
                hops[way, hop, chunk].wait_recv()
                hops[way, hop + 1, chunk] = forward(way, hop + 1, chunk)

    def far_at(way, ahead):
        return (way * (REACH - 1) + ahead - 1) * per if ahead < REACH else 2 * (REACH - 1) * per

    relays, onehots = {}, {}
    for chunk, (begin, size) in enumerate(chunks):
        for way in range(2):
            hops[way, REACH, chunk].wait_recv()
            held = near_at(way, REACH)
            if chunk == 0:
                code = codes_of(near[held : held + mrows, :LANES])
                index = lax.broadcasted_iota(jnp.int32, (REACH * per, mrows), 0)
                ahead = index // per + 1
                goal = plane + (ahead if way == 0 else planes - ahead)
                goal = jnp.where(goal >= planes, goal - planes, goal)
                want = goal * per + index % per + 1
                onehots[way] = as_onehot(code == want.astype(jnp.float32))
            comp[way * REACH * per : (way + 1) * REACH * per, begin : begin + size] = pick_rows(
                onehots[way], near[held : held + mrows, begin : begin + size]
            ).astype(jnp.bfloat16)
            for ahead in range(REACH, 0, -1):
                if ahead == REACH and chunk * 2 // CHUNKS != way:
                    continue
                relays[way, ahead, chunk] = pass_on(
                    comp.at[pl.ds((way * REACH + ahead - 1) * per, per), pl.ds(begin, size)],
                    far_rows.at[pl.ds(far_at(way, ahead), per), pl.ds(begin, size)],
                    fsend,
                    frecv,
                    (way * REACH + ahead - 1) * CHUNKS + chunk,
                    along(ahead - 2 * way * ahead),
                )

    slots = per * planes
    each = slots // PLANE

    def wanted(columns):
        index = lax.broadcasted_iota(jnp.int32, (slots, columns), 0)
        column = lax.broadcasted_iota(jnp.int32, (slots, columns), 1)
        return index % each // 2, index // each * 2 + index % 2, column

    base = plane * per + 1
    group, local, column = wanted(mrows)
    code = codes_of(r_ref[:, :LANES])
    own_hot = as_onehot((group == 0) & (code == (local + base).astype(jnp.float32)))
    group, local, column = wanted(2 * REACH * mrows)
    code = codes_of(near[:, :LANES])
    near_hot = as_onehot(
        (group == 1 + column // mrows) & (code == (local + base).astype(jnp.float32))
    )
    group, local, column = wanted(far_rows.shape[0])
    far_hot = as_onehot((group == 1 + 2 * REACH + column // per) & (local == column % per))

    spread = {}
    mine = pl.ds(pl.multiple_of(spot * each, each), each)
    for chunk, (begin, size) in enumerate(chunks):
        cols = slice(begin, begin + size)
        found = pick_rows(own_hot, r_ref[:, cols]) + pick_rows(near_hot, near[:, cols])
        for way in range(2):
            for ahead in range(1, REACH + 1):
                if (way, ahead, chunk) in relays:
                    relays[way, ahead, chunk].wait_recv()
        ordered[:, cols] = (found + pick_rows(far_hot, far_rows[:, cols])).astype(jnp.bfloat16)
        for distance in range(1, PLANE):
            theirs = pl.ds(pl.multiple_of(lax.rem(spot + distance, PLANE) * each, each), each)
            spread[distance, chunk] = pass_on(
                ordered.at[theirs, pl.ds(begin, size)],
                landed.at[mine, pl.ds(begin, size)],
                psend,
                precv,
                (distance - 1) * CHUNKS + chunk,
                within(distance),
            )
        landed[mine, cols] = ordered[mine, cols]

    for chunk, (begin, size) in enumerate(chunks):
        for distance in range(1, PLANE):
            spread[distance, chunk].wait_recv()
        if chunk == 0:
            tag = to_row(landed[:, :LANES].astype(jnp.float32)[:, 0:1])
            index = lax.broadcasted_iota(jnp.int32, (out_ref.shape[0], slots), 0) + 1
            place = as_onehot(index.astype(jnp.float32) == tag)
            begin, size = begin + LANES, size - LANES
        out_ref[:, begin - LANES : begin - LANES + size] = pick_rows(
            place, landed[:, begin : begin + size]
        ).astype(jnp.bfloat16)
    for copy in started:
        copy.wait_send()


def per_device(segment_ids, block_mask, queries, keys, values, tokens, out_weight, owners, offsets):
    rows = queries.shape[0]
    width = tokens.shape[1]
    nblk = lax.axis_size("blk")
    mrows = rows // 4
    capacity = 2 * mrows
    wide = 4 * width + LANES
    per = 2 * PLANE
    operands = (
        queries,
        keys,
        values,
        segment_ids.reshape(-1, LANES),
        block_mask,
        tokens,
        out_weight,
        owners.reshape(1, mrows),
        offsets.reshape(1, mrows),
    )
    halo = pltpu.VMEM((2 * SPAN,) + keys.shape, keys.dtype)
    dma = pltpu.SemaphoreType.DMA

    def held(count):
        return pltpu.VMEM((count, wide), tokens.dtype)

    return pl.pallas_call(
        program_kernel,
        out_shape=jax.ShapeDtypeStruct((capacity, 4 * width), tokens.dtype),
        in_specs=[pl.BlockSpec(memory_space=pl.ANY)] * len(operands),
        out_specs=pl.BlockSpec(memory_space=pltpu.VMEM),
        scratch_shapes=[pltpu.VMEM(x.shape, x.dtype) for x in operands]
        + [
            halo,
            halo,
            pltpu.VMEM((HEADS, rows, 1), jnp.float32),
            pltpu.VMEM((HEADS, rows, 1), jnp.float32),
            pltpu.VMEM((HEADS, rows, 2 * LANES), jnp.float32),
            held(mrows),
            held(2 * REACH * mrows),
            held(2 * REACH * per),
            held((2 * REACH - 1) * per),
            held(2 * nblk),
            held(2 * nblk),
            dma((len(operands),)),
        ]
        + [dma((2 * SPAN * PARTS,))] * 4
        + [dma((2 * REACH * CHUNKS,))] * 4
        + [dma(((PLANE - 1) * CHUNKS,))] * 2,
        compiler_params=pltpu.CompilerParams(
            collective_id=0, has_side_effects=True, vmem_limit_bytes=56 * 2**20
        ),
    )(*operands)


def solution(mesh):
    placed = (
        P("rep"),
        P("rep", None),
        P(("rep", "blk"), None),
        P(("rep", "blk"), None),
        P(("rep", "blk"), None),
        P(("rep", "blk"), None),
        P(),
        P(("rep", "blk")),
        P(("rep", "blk")),
    )
    return jax.shard_map(
        per_device, mesh=mesh, in_specs=placed, out_specs=P(("rep", "blk"), None), check_vma=False
    )
```

```python
import functools

import jax
import jax.numpy as jnp
from jax import lax
from jax.experimental import pallas as pl
from jax.experimental.pallas import tpu as pltpu
from jax.sharding import PartitionSpec as P

HEADS = 8
SPAN = 3
NEG = -1e30
LANES = 128
PLANE = 8
REACH = 4
CHUNKS = 5
PARTS = 2


def to_column(row):
    size = row.shape[1]
    diagonal = lax.broadcasted_iota(jnp.int32, (size, size), 0) == lax.broadcasted_iota(
        jnp.int32, (size, size), 1
    )
    return jnp.sum(jnp.where(diagonal, row, 0), axis=1, keepdims=True)


def to_row(column):
    size = column.shape[0]
    diagonal = lax.broadcasted_iota(jnp.int32, (size, size), 0) == lax.broadcasted_iota(
        jnp.int32, (size, size), 1
    )
    return jnp.sum(jnp.where(diagonal, column, 0.0), axis=0, keepdims=True)


def codes_of(tags):
    return to_row(tags.astype(jnp.float32)[:, LANES // 2 : LANES // 2 + 1])


def as_onehot(hit):
    return jnp.where(hit, 1.0, 0.0).astype(jnp.bfloat16)


def pick_rows(onehot, rows):
    return jnp.dot(onehot, rows, preferred_element_type=jnp.float32)


def program_kernel(
    q_hbm, k_hbm, v_hbm, seg_hbm, mask_hbm, tok_hbm, w_hbm, owner_hbm, offset_hbm, out_ref,
    q_ref, k_ref, v_ref, seg_ref, mask_ref, tok_ref, w_ref, owner_ref, offset_ref,
    kh, vh, peaks, totals, mixed, r_ref, near, comp, far_rows, ordered, landed,
    loads, ksend, vsend, krecv, vrecv, nsend, nrecv, fsend, frecv, psend, precv,
):
    rows, features = q_ref.shape
    nblk = mask_ref.shape[0]
    width = tok_ref.shape[1]
    hdim = features // HEADS
    block = lax.axis_index("blk")
    scale = 1.0 / jnp.sqrt(jnp.float32(hdim))

    pairs = [
        (q_hbm, q_ref),
        (k_hbm, k_ref),
        (v_hbm, v_ref),
        (seg_hbm, seg_ref),
        (mask_hbm, mask_ref),
        (owner_hbm, owner_ref),
        (offset_hbm, offset_ref),
        (tok_hbm, tok_ref),
        (w_hbm, w_ref),
    ]
    local = [pltpu.make_async_copy(src, dst, loads.at[n]) for n, (src, dst) in enumerate(pairs)]
    for copy in local:
        copy.start()

    rungs = nblk // 2
    rung, side = lax.div(block, 2), lax.rem(block, 2)
    up = lax.rem(rung + 1, rungs) * 2 + side
    down = lax.rem(rung + rungs - 1, rungs) * 2 + side
    across = rung * 2 + 1 - side
    far = lax.rem(rung + 1 - 2 * side + rungs, rungs) * 2 + side
    back = lax.rem(rung - 1 + 2 * side + rungs, rungs) * 2 + side

    planes = nblk // PLANE
    plane, spot = lax.div(block, PLANE), lax.rem(block, PLANE)

    def along(distance):
        return lax.rem(plane + distance + planes, planes) * PLANE + spot

    def within(distance):
        return plane * PLANE + lax.rem(spot + distance, PLANE)

    barrier = pltpu.get_barrier_semaphore()
    peers = [up, down, across]
    peers += [along(d) for k in range(1, REACH + 1) for d in (k, -k)]
    peers += [within(d) for d in range(1, PLANE)]
    for other in peers:
        pl.semaphore_signal(barrier, inc=1, device_id={"blk": other}, device_id_type=pl.DeviceIdType.MESH)
    pl.semaphore_wait(barrier, len(peers))

    half = rows // PARTS
    started = []

    def send(src, dst, sends, recvs, number, slot, part, target):
        span = pl.ds(part * half, half)
        copy = pltpu.make_async_remote_copy(
            src_ref=src.at[span],
            dst_ref=dst.at[slot, span],
            send_sem=sends.at[number * PARTS + part],
            recv_sem=recvs.at[slot * PARTS + part],
            device_id={"blk": target},
            device_id_type=pl.DeviceIdType.MESH,
        )
        copy.start()
        started.append(copy)

    def arrived(dst, recvs, slot, part):
        span = pl.ds(part * half, half)
        pltpu.make_async_copy(
            dst.at[slot, span], dst.at[slot, span], recvs.at[slot * PARTS + part]
        ).wait()

    for part in range(PARTS):
        send(v_hbm, vh, vsend, vrecv, 0, 2 + side, part, across)
        send(k_hbm, kh, ksend, krecv, 1, 4 - 3 * side, part, back)
        send(k_hbm, kh, ksend, krecv, 2, 1 + 3 * side, part, far)
    for part in range(PARTS):
        send(k_hbm, kh, ksend, krecv, 0, 2 + side, part, across)
        send(v_hbm, vh, vsend, vrecv, 2, 1 + 3 * side, part, far)
        send(v_hbm, vh, vsend, vrecv, 1, 4 - 3 * side, part, back)
    for part in range(PARTS):
        arrived(vh, vrecv, 3 - side, part)
        send(vh.at[3 - side], vh, vsend, vrecv, 3, 2 + side, part, far)
        send(vh.at[3 - side], vh, vsend, vrecv, 4, 5 - 5 * side, part, back)
    for part in range(PARTS):
        arrived(kh, krecv, 4 - 3 * side, part)
        send(kh.at[4 - 3 * side], kh, ksend, krecv, 3, 3 - side, part, across)
    for part in range(PARTS):
        arrived(kh, krecv, 1 + 3 * side, part)
        send(kh.at[1 + 3 * side], kh, ksend, krecv, 4, 5 * side, part, across)

    for copy in local:
        copy.wait()

    def ids_of(column):
        halves = rows // LANES
        return jnp.concatenate(
            [seg_ref[pl.ds(column * halves + n, 1), :] for n in range(halves)], axis=1
        )

    query_seg = to_column(ids_of(block))
    mask_row = mask_ref[pl.ds(block, 1), :]
    columns = lax.broadcasted_iota(jnp.int32, mask_row.shape, 1)

    def segments(dist):
        column = block + dist
        flag = jnp.sum(jnp.where(columns == column, mask_row, 0), axis=1, keepdims=True)
        return jnp.where(flag > 0, ids_of(lax.rem(column + nblk, nblk)), -1)

    def window(head):
        first, last = head * hdim, (head + 1) * hdim
        low, high = first // LANES * LANES, -(-last // LANES) * LANES
        lane = lax.broadcasted_iota(jnp.int32, (rows, high - low), 1) + low
        return low, high, (lane >= first) & (lane < last)

    def attend(blocks, fresh):
        for head in range(HEADS):
            low, high, mine = window(head)
            query = jnp.where(mine, q_ref[:, low:high], jnp.bfloat16(0))
            scores = []
            for key, _, key_seg in blocks:
                part = lax.dot_general(
                    query,
                    key[:, low:high],
                    (((1,), (1,)), ((), ())),
                    preferred_element_type=jnp.float32,
                )
                scores.append(jnp.where(query_seg == key_seg, part, NEG))
            peak = jnp.max(functools.reduce(jnp.maximum, scores), axis=1, keepdims=True)
            if fresh:
                total = jnp.zeros((rows, 1), jnp.float32)
                result = jnp.zeros((rows, high - low), jnp.float32)
            else:
                before = peaks[head]
                peak = jnp.maximum(peak, before)
                factor = jnp.exp((before - peak) * scale)
                total = totals[head] * factor
                result = mixed[head, :, : high - low] * factor
            for (_, value, _), part in zip(blocks, scores):
                weights = jnp.exp((part - peak) * scale)
                total = total + jnp.sum(weights, axis=1, keepdims=True)
                result = result + jnp.dot(
                    weights.astype(jnp.bfloat16), value[:, low:high], preferred_element_type=jnp.float32
                )
            peaks[head] = peak
            totals[head] = total
            mixed[head, :, : high - low] = result

    def held(slot, dist):
        return kh.at[slot], vh.at[slot], segments(dist)

    for part in range(PARTS):
        arrived(kh, krecv, 3 - side, part)
        arrived(vh, vrecv, 1, part)
        arrived(vh, vrecv, 4, part)
    attend(
        [(k_ref, v_ref, segments(0)), held(3 - side, 1 - 2 * side), held(1, -2), held(4, 2)], True
    )
    for part in range(PARTS):
        arrived(vh, vrecv, 2 + side, part)
        send(vh.at[2 + side], vh, vsend, vrecv, 5, 5 * side, part, far)
    for part in range(PARTS):
        arrived(kh, krecv, 2 + side, part)
        send(kh.at[2 + side], kh, ksend, krecv, 5, 5 * side, part, far)
    for part in range(PARTS):
        arrived(vh, vrecv, 5 - 5 * side, part)
        arrived(kh, krecv, 5 - 5 * side, part)
    attend([held(2 + side, 2 * side - 1), held(5 - 5 * side, 3 - 6 * side)], False)
    owner_row = owner_ref[...]
    mrows, wide = r_ref.shape
    earlier = (to_column(owner_row) == owner_row) & (
        lax.broadcasted_iota(jnp.int32, (mrows, mrows), 0)
        < lax.broadcasted_iota(jnp.int32, (mrows, mrows), 1)
    )
    rank = jnp.sum(earlier.astype(jnp.int32), axis=0, keepdims=True)
    lane = lax.broadcasted_iota(jnp.int32, (mrows, LANES), 1)
    offset, code = to_column(offset_ref[...]), to_column(2 * owner_row + rank)
    tags = jnp.where(lane < LANES // 2, offset + 1, code + 1)
    r_ref[:, :LANES] = tags.astype(jnp.float32).astype(jnp.bfloat16)
    for part in range(PARTS):
        arrived(vh, vrecv, 5 * side, part)
        arrived(kh, krecv, 5 * side, part)
    attend([held(5 * side, 6 * side - 3)], False)

    pieces = []
    for group in range(features // LANES):
        piece = jnp.zeros((rows, LANES), jnp.float32)
        for head in range(HEADS):
            low, high, mine = window(head)
            start = group * LANES - low
            if 0 <= start < high - low:
                ready = mixed[head, :, start : start + LANES] / totals[head]
                piece = jnp.where(mine[:, start : start + LANES], ready, piece)
        pieces.append(piece.astype(jnp.bfloat16))
    attended = jnp.concatenate(pieces, axis=1)
    hidden = (
        tok_ref[...].astype(jnp.float32)
        + jnp.dot(attended, w_ref[...], preferred_element_type=jnp.float32)
    ).astype(jnp.bfloat16)
    merged = lax.broadcasted_iota(jnp.int32, (mrows, rows), 0)
    source = lax.broadcasted_iota(jnp.int32, (mrows, rows), 1)
    per = 2 * PLANE
    step = (wide - LANES) // CHUNKS
    chunks = [(0, LANES + step)] + [(LANES + c * step, step) for c in range(1, CHUNKS)]

    def pass_on(src, dst, sends, recvs, number, target):
        copy = pltpu.make_async_remote_copy(
            src_ref=src,
            dst_ref=dst,
            send_sem=sends.at[number],
            recv_sem=recvs.at[number],
            device_id={"blk": target},
            device_id_type=pl.DeviceIdType.MESH,
        )
        copy.start()
        started.append(copy)
        return copy

    def near_at(way, hop):
        return (way * REACH + hop - 1) * mrows

    def forward(way, hop, chunk):
        begin, size = chunks[chunk]
        cols = pl.ds(begin, size)
        src = r_ref.at[:, cols] if hop == 1 else near.at[pl.ds(near_at(way, hop - 1), mrows), cols]
        return pass_on(
            src,
            near.at[pl.ds(near_at(way, hop), mrows), cols],
            nsend,
            nrecv,
            (way * REACH + hop - 1) * CHUNKS + chunk,
            along(1 - 2 * way),
        )

    hops = {}
    built = 0
    for quarter in range(4):
        pick = source == 4 * merged + quarter
        built = LANES + (quarter + 1) * width
        r_ref[:, built - width : built] = pick_rows(as_onehot(pick), hidden).astype(jnp.bfloat16)
        for chunk, (begin, size) in enumerate(chunks):
            if built - width < begin + size <= built:
                for way in range(2):
                    hops[way, 1, chunk] = forward(way, 1, chunk)
    for hop in range(1, REACH):
        for chunk in range(CHUNKS):
            for way in range(2):
                hops[way, hop, chunk].wait_recv()
                hops[way, hop + 1, chunk] = forward(way, hop + 1, chunk)

    def far_at(way, ahead):
        return (way * (REACH - 1) + ahead - 1) * per if ahead < REACH else 2 * (REACH - 1) * per

    relays, onehots = {}, {}
    for chunk, (begin, size) in enumerate(chunks):
        for way in range(2):
            hops[way, REACH, chunk].wait_recv()
            held = near_at(way, REACH)
            if chunk == 0:
                code = codes_of(near[held : held + mrows, :LANES])
                index = lax.broadcasted_iota(jnp.int32, (REACH * per, mrows), 0)
                ahead = index // per + 1
                goal = plane + (ahead if way == 0 else planes - ahead)
                goal = jnp.where(goal >= planes, goal - planes, goal)
                want = goal * per + index % per + 1
                onehots[way] = as_onehot(code == want.astype(jnp.float32))
            comp[way * REACH * per : (way + 1) * REACH * per, begin : begin + size] = pick_rows(
                onehots[way], near[held : held + mrows, begin : begin + size]
            ).astype(jnp.bfloat16)
            for ahead in range(REACH, 0, -1):
                if ahead == REACH and chunk * 2 // CHUNKS != way:
                    continue
                relays[way, ahead, chunk] = pass_on(
                    comp.at[pl.ds((way * REACH + ahead - 1) * per, per), pl.ds(begin, size)],
                    far_rows.at[pl.ds(far_at(way, ahead), per), pl.ds(begin, size)],
                    fsend,
                    frecv,
                    (way * REACH + ahead - 1) * CHUNKS + chunk,
                    along(ahead - 2 * way * ahead),
                )

    slots = per * planes
    each = slots // PLANE

    def wanted(columns):
        index = lax.broadcasted_iota(jnp.int32, (slots, columns), 0)
        column = lax.broadcasted_iota(jnp.int32, (slots, columns), 1)
        return index % each // 2, index // each * 2 + index % 2, column

    base = plane * per + 1
    group, local, column = wanted(mrows)
    code = codes_of(r_ref[:, :LANES])
    own_hot = as_onehot((group == 0) & (code == (local + base).astype(jnp.float32)))
    group, local, column = wanted(2 * REACH * mrows)
    code = codes_of(near[:, :LANES])
    near_hot = as_onehot(
        (group == 1 + column // mrows) & (code == (local + base).astype(jnp.float32))
    )
    group, local, column = wanted(far_rows.shape[0])
    far_hot = as_onehot((group == 1 + 2 * REACH + column // per) & (local == column % per))

    spread = {}
    mine = pl.ds(pl.multiple_of(spot * each, each), each)
    for chunk, (begin, size) in enumerate(chunks):
        cols = slice(begin, begin + size)
        found = pick_rows(own_hot, r_ref[:, cols]) + pick_rows(near_hot, near[:, cols])
        for way in range(2):
            for ahead in range(1, REACH + 1):
                if (way, ahead, chunk) in relays:
                    relays[way, ahead, chunk].wait_recv()
        ordered[:, cols] = (found + pick_rows(far_hot, far_rows[:, cols])).astype(jnp.bfloat16)
        for distance in range(1, PLANE):
            theirs = pl.ds(pl.multiple_of(lax.rem(spot + distance, PLANE) * each, each), each)
            spread[distance, chunk] = pass_on(
                ordered.at[theirs, pl.ds(begin, size)],
                landed.at[mine, pl.ds(begin, size)],
                psend,
                precv,
                (distance - 1) * CHUNKS + chunk,
                within(distance),
            )
        landed[mine, cols] = ordered[mine, cols]

    for chunk, (begin, size) in enumerate(chunks):
        for distance in range(1, PLANE):
            spread[distance, chunk].wait_recv()
        if chunk == 0:
            tag = to_row(landed[:, :LANES].astype(jnp.float32)[:, 0:1])
            index = lax.broadcasted_iota(jnp.int32, (out_ref.shape[0], slots), 0) + 1
            place = as_onehot(index.astype(jnp.float32) == tag)
            begin, size = begin + LANES, size - LANES
        out_ref[:, begin - LANES : begin - LANES + size] = pick_rows(
            place, landed[:, begin : begin + size]
        ).astype(jnp.bfloat16)
    for copy in started:
        copy.wait_send()


def per_device(segment_ids, block_mask, queries, keys, values, tokens, out_weight, owners, offsets):
    rows = queries.shape[0]
    width = tokens.shape[1]
    nblk = lax.axis_size("blk")
    mrows = rows // 4
    capacity = 2 * mrows
    wide = 4 * width + LANES
    per = 2 * PLANE
    operands = (
        queries,
        keys,
        values,
        segment_ids.reshape(-1, LANES),
        block_mask,
        tokens,
        out_weight,
        owners.reshape(1, mrows),
        offsets.reshape(1, mrows),
    )
    halo = pltpu.VMEM((2 * SPAN,) + keys.shape, keys.dtype)
    dma = pltpu.SemaphoreType.DMA

    def held(count):
        return pltpu.VMEM((count, wide), tokens.dtype)

    return pl.pallas_call(
        program_kernel,
        out_shape=jax.ShapeDtypeStruct((capacity, 4 * width), tokens.dtype),
        in_specs=[pl.BlockSpec(memory_space=pl.ANY)] * len(operands),
        out_specs=pl.BlockSpec(memory_space=pltpu.VMEM),
        scratch_shapes=[pltpu.VMEM(x.shape, x.dtype) for x in operands]
        + [
            halo,
            halo,
            pltpu.VMEM((HEADS, rows, 1), jnp.float32),
            pltpu.VMEM((HEADS, rows, 1), jnp.float32),
            pltpu.VMEM((HEADS, rows, 2 * LANES), jnp.float32),
            held(mrows),
            held(2 * REACH * mrows),
            held(2 * REACH * per),
            held((2 * REACH - 1) * per),
            held(2 * nblk),
            held(2 * nblk),
            dma((len(operands),)),
        ]
        + [dma((2 * SPAN * PARTS,))] * 4
        + [dma((2 * REACH * CHUNKS,))] * 4
        + [dma(((PLANE - 1) * CHUNKS,))] * 2,
        compiler_params=pltpu.CompilerParams(
            collective_id=0, has_side_effects=True, vmem_limit_bytes=56 * 2**20
        ),
    )(*operands)


def solution(mesh):
    placed = (
        P("rep"),
        P("rep", None),
        P(("rep", "blk"), None),
        P(("rep", "blk"), None),
        P(("rep", "blk"), None),
        P(("rep", "blk"), None),
        P(),
        P(("rep", "blk")),
        P(("rep", "blk")),
    )
    return jax.shard_map(
        per_device, mesh=mesh, in_specs=placed, out_specs=P(("rep", "blk"), None), check_vma=False
    )
```

```python
import functools

import jax
import jax.numpy as jnp
from jax import lax
from jax.experimental import pallas as pl
from jax.experimental.pallas import tpu as pltpu
from jax.sharding import PartitionSpec as P

HEADS = 8
SPAN = 3
NEG = -1e30
LANES = 128
PLANE = 8
REACH = 4
CHUNKS = 8
PARTS = 2


def to_column(row):
    size = row.shape[1]
    diagonal = lax.broadcasted_iota(jnp.int32, (size, size), 0) == lax.broadcasted_iota(
        jnp.int32, (size, size), 1
    )
    return jnp.sum(jnp.where(diagonal, row, 0), axis=1, keepdims=True)


def to_row(column):
    size = column.shape[0]
    diagonal = lax.broadcasted_iota(jnp.int32, (size, size), 0) == lax.broadcasted_iota(
        jnp.int32, (size, size), 1
    )
    return jnp.sum(jnp.where(diagonal, column, 0.0), axis=0, keepdims=True)


def codes_of(tags):
    return to_row(tags.astype(jnp.float32)[:, LANES // 2 : LANES // 2 + 1])


def as_onehot(hit):
    return jnp.where(hit, 1.0, 0.0).astype(jnp.bfloat16)


def pick_rows(onehot, rows):
    return jnp.dot(onehot, rows, preferred_element_type=jnp.float32)


def program_kernel(
    q_hbm, k_hbm, v_hbm, seg_hbm, mask_hbm, tok_hbm, w_hbm, owner_hbm, offset_hbm, out_ref,
    q_ref, k_ref, v_ref, seg_ref, mask_ref, tok_ref, w_ref, owner_ref, offset_ref,
    kh, vh, peaks, totals, mixed, r_ref, near, comp, far_rows, ordered, landed,
    loads, ksend, vsend, krecv, vrecv, nsend, nrecv, fsend, frecv, psend, precv,
):
    rows, features = q_ref.shape
    nblk = mask_ref.shape[0]
    width = tok_ref.shape[1]
    hdim = features // HEADS
    block = lax.axis_index("blk")
    scale = 1.0 / jnp.sqrt(jnp.float32(hdim))

    pairs = [
        (q_hbm, q_ref),
        (k_hbm, k_ref),
        (v_hbm, v_ref),
        (seg_hbm, seg_ref),
        (mask_hbm, mask_ref),
        (owner_hbm, owner_ref),
        (offset_hbm, offset_ref),
        (tok_hbm, tok_ref),
        (w_hbm, w_ref),
    ]
    local = [pltpu.make_async_copy(src, dst, loads.at[n]) for n, (src, dst) in enumerate(pairs)]
    for copy in local:
        copy.start()

    rungs = nblk // 2
    rung, side = lax.div(block, 2), lax.rem(block, 2)
    up = lax.rem(rung + 1, rungs) * 2 + side
    down = lax.rem(rung + rungs - 1, rungs) * 2 + side
    across = rung * 2 + 1 - side
    far = lax.rem(rung + 1 - 2 * side + rungs, rungs) * 2 + side
    back = lax.rem(rung - 1 + 2 * side + rungs, rungs) * 2 + side

    planes = nblk // PLANE
    plane, spot = lax.div(block, PLANE), lax.rem(block, PLANE)

    def along(distance):
        return lax.rem(plane + distance + planes, planes) * PLANE + spot

    def within(distance):
        return plane * PLANE + lax.rem(spot + distance, PLANE)

    barrier = pltpu.get_barrier_semaphore()
    peers = [up, down, across]
    peers += [along(d) for k in range(1, REACH + 1) for d in (k, -k)]
    peers += [within(d) for d in range(1, PLANE)]
    for other in peers:
        pl.semaphore_signal(barrier, inc=1, device_id={"blk": other}, device_id_type=pl.DeviceIdType.MESH)
    pl.semaphore_wait(barrier, len(peers))

    half = rows // PARTS
    started = []

    def send(src, dst, sends, recvs, number, slot, part, target):
        span = pl.ds(part * half, half)
        copy = pltpu.make_async_remote_copy(
            src_ref=src.at[span],
            dst_ref=dst.at[slot, span],
            send_sem=sends.at[number * PARTS + part],
            recv_sem=recvs.at[slot * PARTS + part],
            device_id={"blk": target},
            device_id_type=pl.DeviceIdType.MESH,
        )
        copy.start()
        started.append(copy)

    def arrived(dst, recvs, slot, part):
        span = pl.ds(part * half, half)
        pltpu.make_async_copy(
            dst.at[slot, span], dst.at[slot, span], recvs.at[slot * PARTS + part]
        ).wait()

    for part in range(PARTS):
        send(v_hbm, vh, vsend, vrecv, 0, 2 + side, part, across)
        send(k_hbm, kh, ksend, krecv, 1, 4 - 3 * side, part, back)
        send(k_hbm, kh, ksend, krecv, 2, 1 + 3 * side, part, far)
    for part in range(PARTS):
        send(k_hbm, kh, ksend, krecv, 0, 2 + side, part, across)
        send(v_hbm, vh, vsend, vrecv, 2, 1 + 3 * side, part, far)
        send(v_hbm, vh, vsend, vrecv, 1, 4 - 3 * side, part, back)
    for part in range(PARTS):
        arrived(vh, vrecv, 3 - side, part)
        send(vh.at[3 - side], vh, vsend, vrecv, 3, 2 + side, part, far)
        send(vh.at[3 - side], vh, vsend, vrecv, 4, 5 - 5 * side, part, back)
    for part in range(PARTS):
        arrived(kh, krecv, 4 - 3 * side, part)
        send(kh.at[4 - 3 * side], kh, ksend, krecv, 3, 3 - side, part, across)
    for part in range(PARTS):
        arrived(kh, krecv, 1 + 3 * side, part)
        send(kh.at[1 + 3 * side], kh, ksend, krecv, 4, 5 * side, part, across)

    for copy in local:
        copy.wait()

    def ids_of(column):
        halves = rows // LANES
        return jnp.concatenate(
            [seg_ref[pl.ds(column * halves + n, 1), :] for n in range(halves)], axis=1
        )

    query_seg = to_column(ids_of(block))
    mask_row = mask_ref[pl.ds(block, 1), :]
    columns = lax.broadcasted_iota(jnp.int32, mask_row.shape, 1)

    def segments(dist):
        column = block + dist
        flag = jnp.sum(jnp.where(columns == column, mask_row, 0), axis=1, keepdims=True)
        return jnp.where(flag > 0, ids_of(lax.rem(column + nblk, nblk)), -1)

    def window(head):
        first, last = head * hdim, (head + 1) * hdim
        low, high = first // LANES * LANES, -(-last // LANES) * LANES
        lane = lax.broadcasted_iota(jnp.int32, (rows, high - low), 1) + low
        return low, high, (lane >= first) & (lane < last)

    def attend(blocks, fresh):
        for head in range(HEADS):
            low, high, mine = window(head)
            query = jnp.where(mine, q_ref[:, low:high], jnp.bfloat16(0))
            scores = []
            for key, _, key_seg in blocks:
                part = lax.dot_general(
                    query,
                    key[:, low:high],
                    (((1,), (1,)), ((), ())),
                    preferred_element_type=jnp.float32,
                )
                scores.append(jnp.where(query_seg == key_seg, part, NEG))
            peak = jnp.max(functools.reduce(jnp.maximum, scores), axis=1, keepdims=True)
            if fresh:
                total = jnp.zeros((rows, 1), jnp.float32)
                result = jnp.zeros((rows, high - low), jnp.float32)
            else:
                before = peaks[head]
                peak = jnp.maximum(peak, before)
                factor = jnp.exp((before - peak) * scale)
                total = totals[head] * factor
                result = mixed[head, :, : high - low] * factor
            for (_, value, _), part in zip(blocks, scores):
                weights = jnp.exp((part - peak) * scale)
                total = total + jnp.sum(weights, axis=1, keepdims=True)
                result = result + jnp.dot(
                    weights.astype(jnp.bfloat16), value[:, low:high], preferred_element_type=jnp.float32
                )
            peaks[head] = peak
            totals[head] = total
            mixed[head, :, : high - low] = result

    def held(slot, dist):
        return kh.at[slot], vh.at[slot], segments(dist)

    for part in range(PARTS):
        arrived(kh, krecv, 3 - side, part)
        arrived(vh, vrecv, 1, part)
        arrived(vh, vrecv, 4, part)
    attend(
        [(k_ref, v_ref, segments(0)), held(3 - side, 1 - 2 * side), held(1, -2), held(4, 2)], True
    )
    for part in range(PARTS):
        arrived(vh, vrecv, 2 + side, part)
        send(vh.at[2 + side], vh, vsend, vrecv, 5, 5 * side, part, far)
    for part in range(PARTS):
        arrived(kh, krecv, 2 + side, part)
        send(kh.at[2 + side], kh, ksend, krecv, 5, 5 * side, part, far)
    for part in range(PARTS):
        arrived(vh, vrecv, 5 - 5 * side, part)
        arrived(kh, krecv, 5 - 5 * side, part)
    attend([held(2 + side, 2 * side - 1), held(5 - 5 * side, 3 - 6 * side)], False)
    owner_row = owner_ref[...]
    mrows, wide = r_ref.shape
    earlier = (to_column(owner_row) == owner_row) & (
        lax.broadcasted_iota(jnp.int32, (mrows, mrows), 0)
        < lax.broadcasted_iota(jnp.int32, (mrows, mrows), 1)
    )
    rank = jnp.sum(earlier.astype(jnp.int32), axis=0, keepdims=True)
    lane = lax.broadcasted_iota(jnp.int32, (mrows, LANES), 1)
    offset, code = to_column(offset_ref[...]), to_column(2 * owner_row + rank)
    tags = jnp.where(lane < LANES // 2, offset + 1, code + 1)
    r_ref[:, :LANES] = tags.astype(jnp.float32).astype(jnp.bfloat16)
    for part in range(PARTS):
        arrived(vh, vrecv, 5 * side, part)
        arrived(kh, krecv, 5 * side, part)
    attend([held(5 * side, 6 * side - 3)], False)

    pieces = []
    for group in range(features // LANES):
        piece = jnp.zeros((rows, LANES), jnp.float32)
        for head in range(HEADS):
            low, high, mine = window(head)
            start = group * LANES - low
            if 0 <= start < high - low:
                ready = mixed[head, :, start : start + LANES] / totals[head]
                piece = jnp.where(mine[:, start : start + LANES], ready, piece)
        pieces.append(piece.astype(jnp.bfloat16))
    attended = jnp.concatenate(pieces, axis=1)
    hidden = (
        tok_ref[...].astype(jnp.float32)
        + jnp.dot(attended, w_ref[...], preferred_element_type=jnp.float32)
    ).astype(jnp.bfloat16)
    merged = lax.broadcasted_iota(jnp.int32, (mrows, rows), 0)
    source = lax.broadcasted_iota(jnp.int32, (mrows, rows), 1)
    per = 2 * PLANE
    step = (wide - LANES) // CHUNKS
    chunks = [(0, LANES + step)] + [(LANES + c * step, step) for c in range(1, CHUNKS)]

    def pass_on(src, dst, sends, recvs, number, target):
        copy = pltpu.make_async_remote_copy(
            src_ref=src,
            dst_ref=dst,
            send_sem=sends.at[number],
            recv_sem=recvs.at[number],
            device_id={"blk": target},
            device_id_type=pl.DeviceIdType.MESH,
        )
        copy.start()
        started.append(copy)
        return copy

    def near_at(way, hop):
        return (way * REACH + hop - 1) * mrows

    def forward(way, hop, chunk):
        begin, size = chunks[chunk]
        cols = pl.ds(begin, size)
        src = r_ref.at[:, cols] if hop == 1 else near.at[pl.ds(near_at(way, hop - 1), mrows), cols]
        return pass_on(
            src,
            near.at[pl.ds(near_at(way, hop), mrows), cols],
            nsend,
            nrecv,
            (way * REACH + hop - 1) * CHUNKS + chunk,
            along(1 - 2 * way),
        )

    hops = {}
    built = 0
    for quarter in range(4):
        pick = source == 4 * merged + quarter
        built = LANES + (quarter + 1) * width
        r_ref[:, built - width : built] = pick_rows(as_onehot(pick), hidden).astype(jnp.bfloat16)
        for chunk, (begin, size) in enumerate(chunks):
            if built - width < begin + size <= built:
                for way in range(2):
                    hops[way, 1, chunk] = forward(way, 1, chunk)
    for hop in range(1, REACH):
        for chunk in range(CHUNKS):
            for way in range(2):
                hops[way, hop, chunk].wait_recv()
                hops[way, hop + 1, chunk] = forward(way, hop + 1, chunk)

    def far_at(way, ahead):
        return (way * (REACH - 1) + ahead - 1) * per if ahead < REACH else 2 * (REACH - 1) * per

    relays, onehots = {}, {}
    for chunk, (begin, size) in enumerate(chunks):
        for way in range(2):
            hops[way, REACH, chunk].wait_recv()
            held = near_at(way, REACH)
            if chunk == 0:
                code = codes_of(near[held : held + mrows, :LANES])
                index = lax.broadcasted_iota(jnp.int32, (REACH * per, mrows), 0)
                ahead = index // per + 1
                goal = plane + (ahead if way == 0 else planes - ahead)
                goal = jnp.where(goal >= planes, goal - planes, goal)
                want = goal * per + index % per + 1
                onehots[way] = as_onehot(code == want.astype(jnp.float32))
            comp[way * REACH * per : (way + 1) * REACH * per, begin : begin + size] = pick_rows(
                onehots[way], near[held : held + mrows, begin : begin + size]
            ).astype(jnp.bfloat16)
            for ahead in range(REACH, 0, -1):
                if ahead == REACH and chunk * 2 // CHUNKS != way:
                    continue
                relays[way, ahead, chunk] = pass_on(
                    comp.at[pl.ds((way * REACH + ahead - 1) * per, per), pl.ds(begin, size)],
                    far_rows.at[pl.ds(far_at(way, ahead), per), pl.ds(begin, size)],
                    fsend,
                    frecv,
                    (way * REACH + ahead - 1) * CHUNKS + chunk,
                    along(ahead - 2 * way * ahead),
                )

    slots = per * planes
    each = slots // PLANE

    def wanted(columns):
        index = lax.broadcasted_iota(jnp.int32, (slots, columns), 0)
        column = lax.broadcasted_iota(jnp.int32, (slots, columns), 1)
        return index % each // 2, index // each * 2 + index % 2, column

    base = plane * per + 1
    group, local, column = wanted(mrows)
    code = codes_of(r_ref[:, :LANES])
    own_hot = as_onehot((group == 0) & (code == (local + base).astype(jnp.float32)))
    group, local, column = wanted(2 * REACH * mrows)
    code = codes_of(near[:, :LANES])
    near_hot = as_onehot(
        (group == 1 + column // mrows) & (code == (local + base).astype(jnp.float32))
    )
    group, local, column = wanted(far_rows.shape[0])
    far_hot = as_onehot((group == 1 + 2 * REACH + column // per) & (local == column % per))

    spread = {}
    mine = pl.ds(pl.multiple_of(spot * each, each), each)
    for chunk, (begin, size) in enumerate(chunks):
        cols = slice(begin, begin + size)
        found = pick_rows(own_hot, r_ref[:, cols]) + pick_rows(near_hot, near[:, cols])
        for way in range(2):
            for ahead in range(1, REACH + 1):
                if (way, ahead, chunk) in relays:
                    relays[way, ahead, chunk].wait_recv()
        ordered[:, cols] = (found + pick_rows(far_hot, far_rows[:, cols])).astype(jnp.bfloat16)
        for distance in range(1, PLANE):
            theirs = pl.ds(pl.multiple_of(lax.rem(spot + distance, PLANE) * each, each), each)
            spread[distance, chunk] = pass_on(
                ordered.at[theirs, pl.ds(begin, size)],
                landed.at[mine, pl.ds(begin, size)],
                psend,
                precv,
                (distance - 1) * CHUNKS + chunk,
                within(distance),
            )
        landed[mine, cols] = ordered[mine, cols]

    for chunk, (begin, size) in enumerate(chunks):
        for distance in range(1, PLANE):
            spread[distance, chunk].wait_recv()
        if chunk == 0:
            tag = to_row(landed[:, :LANES].astype(jnp.float32)[:, 0:1])
            index = lax.broadcasted_iota(jnp.int32, (out_ref.shape[0], slots), 0) + 1
            place = as_onehot(index.astype(jnp.float32) == tag)
            begin, size = begin + LANES, size - LANES
        out_ref[:, begin - LANES : begin - LANES + size] = pick_rows(
            place, landed[:, begin : begin + size]
        ).astype(jnp.bfloat16)
    for copy in started:
        copy.wait_send()


def per_device(segment_ids, block_mask, queries, keys, values, tokens, out_weight, owners, offsets):
    rows = queries.shape[0]
    width = tokens.shape[1]
    nblk = lax.axis_size("blk")
    mrows = rows // 4
    capacity = 2 * mrows
    wide = 4 * width + LANES
    per = 2 * PLANE
    operands = (
        queries,
        keys,
        values,
        segment_ids.reshape(-1, LANES),
        block_mask,
        tokens,
        out_weight,
        owners.reshape(1, mrows),
        offsets.reshape(1, mrows),
    )
    halo = pltpu.VMEM((2 * SPAN,) + keys.shape, keys.dtype)
    dma = pltpu.SemaphoreType.DMA

    def held(count):
        return pltpu.VMEM((count, wide), tokens.dtype)

    return pl.pallas_call(
        program_kernel,
        out_shape=jax.ShapeDtypeStruct((capacity, 4 * width), tokens.dtype),
        in_specs=[pl.BlockSpec(memory_space=pl.ANY)] * len(operands),
        out_specs=pl.BlockSpec(memory_space=pltpu.VMEM),
        scratch_shapes=[pltpu.VMEM(x.shape, x.dtype) for x in operands]
        + [
            halo,
            halo,
            pltpu.VMEM((HEADS, rows, 1), jnp.float32),
            pltpu.VMEM((HEADS, rows, 1), jnp.float32),
            pltpu.VMEM((HEADS, rows, 2 * LANES), jnp.float32),
            held(mrows),
            held(2 * REACH * mrows),
            held(2 * REACH * per),
            held((2 * REACH - 1) * per),
            held(2 * nblk),
            held(2 * nblk),
            dma((len(operands),)),
        ]
        + [dma((2 * SPAN * PARTS,))] * 4
        + [dma((2 * REACH * CHUNKS,))] * 4
        + [dma(((PLANE - 1) * CHUNKS,))] * 2,
        compiler_params=pltpu.CompilerParams(
            collective_id=0, has_side_effects=True, vmem_limit_bytes=56 * 2**20
        ),
    )(*operands)


def solution(mesh):
    placed = (
        P("rep"),
        P("rep", None),
        P(("rep", "blk"), None),
        P(("rep", "blk"), None),
        P(("rep", "blk"), None),
        P(("rep", "blk"), None),
        P(),
        P(("rep", "blk")),
        P(("rep", "blk")),
    )
    return jax.shard_map(
        per_device, mesh=mesh, in_specs=placed, out_specs=P(("rep", "blk"), None), check_vma=False
    )
```
